256 devices in a mesh: set: 8 (over y_hi, x), exp: 4 (over y_lo, core), seq: 8 (over z).
Axes of the slice: x: 4, y: 4 (y_hi: 2, y_lo: 2; y = y_hi * 2 + y_lo), z: 8, core: 2. Of those that a mesh axis runs over, the one named last changes fastest.
Arguments:
- tokens: bfloat16 [12288, 2560], P(('set', 'exp', 'seq')), parts along dimension 0, may hold values from -6 to 6
- expert_ids: int32 [12288, 2], P(('set', 'exp', 'seq')), parts along dimension 0, may hold values from 0 to 3, as said below
- gate_nums: int32 [12288, 2], P(('set', 'exp', 'seq')), parts along dimension 0, may hold values from 1 to 8
- moe_gain: float32 [2560], replicated, may hold values from 0.1 to 1.9
- w_gate_up: bfloat16 [4, 2560, 2, 3584], P('exp', None, None, 'seq'), may hold values from -0.125 to 0.125
- w_down: bfloat16 [4, 3584, 2560], P('exp', 'seq'), may hold values from -0.09375 to 0.09375
- attn_gain: float32 [2560], replicated, may hold values from 0.1 to 1.9
- w_qkv: bfloat16 [2560, 3, 2048], P(None, None, 'seq'), may hold values from -0.125 to 0.125
- q_gain: float32 [128], replicated, may hold values from 1.2 to 2.2
- k_gain: float32 [128], replicated, may hold values from 1.2 to 2.2
- w_out: bfloat16 [2048, 2560], P('seq'), may hold values from -0.125 to 0.125
Outputs:
- mixed: bfloat16 [12288, 2560], P(('set', 'exp', 'seq')), parts along dimension 0
- attended: bfloat16 [12288, 2560], P(('set', 'exp', 'seq')), parts along dimension 0
The draws below stay inside these ranges and needn't reach their ends.
There are 8 independent parts, one for each index of `set`. The reference program is written for one: setup_inputs(seed, part) draws one part's arguments, and reference() takes and returns one part's arrays. A program takes and returns all parts, laid end to end along the dimension named above; an argument that names none is the same for every part. Nothing has to cross between parts.
Inputs may be any that keep to these rules, and one draw needn't show every extreme that they name: `expert_ids`: the two ids of a row differ. In the rows of one device no expert is named by more than 36 rows, and one expert, the same for all devices of a set, is named by exactly 36 of them.
All inputs are finite; a program needn't handle non-finite values.
Results may differ from the reference program's by a relative error of at most 0.014.
Values may be sent and summed in bfloat16 or wider, within the bound.
No kernel may reach another device: no remote copies, remote signals or barrier semaphores. Data moves between devices by JAX's collectives and lax.ppermute only.
A program may use at most 64 MiB of HBM per device.

```python
import math
import jax
import jax.numpy as jnp
from jax import lax

D = 2560
FF = 3584
EXPERTS = 4
HEADS = 16
HD = 128
TOK_DEV = 48
CAP = 36
TOKENS = 1536
N_SEQ = 8


def draw_expert_ids(key, part):
    blocks = TOKENS // TOK_DEV
    remaining = TOK_DEV - CAP
    subkeys = jax.random.split(key, 4)
    heavy_expert = jax.random.randint(subkeys[0], (), 0, EXPERTS)
    offsets = jax.random.randint(subkeys[1], (blocks, CAP), 1, EXPERTS)
    other_expert = (heavy_expert + offsets) % EXPERTS
    counts = jnp.sum((other_expert[:, :, None] == jnp.arange(EXPERTS)[None, None, :]).astype(jnp.int32), axis=1)
    missing = jnp.argmax(counts, axis=1).astype(jnp.int32)
    offset_step = (missing - heavy_expert) % EXPERTS
    first_rest = (heavy_expert + offset_step % 3 + 1) % EXPERTS
    second_rest = (heavy_expert + (offset_step + 1) % 3 + 1) % EXPERTS
    head_pairs = jnp.stack([jnp.full((blocks, CAP), heavy_expert, jnp.int32), other_expert.astype(jnp.int32)], axis=-1)
    tail_pairs = jnp.stack([jnp.broadcast_to(first_rest[:, None], (blocks, remaining)), jnp.broadcast_to(second_rest[:, None], (blocks, remaining))], axis=-1).astype(jnp.int32)
    expert_pairs = jnp.concatenate([head_pairs, tail_pairs], axis=1)
    flipped = jax.random.randint(subkeys[2], (blocks, TOK_DEV, 1), 0, 2)
    expert_pairs = jnp.where(flipped == 1, expert_pairs[:, :, ::-1], expert_pairs)
    ranking = jax.random.randint(subkeys[3], (blocks, TOK_DEV), 0, 1 << 20) * TOK_DEV + jnp.arange(TOK_DEV)[None, :]
    placing = jnp.argsort(ranking, axis=1)
    expert_pairs = jnp.take_along_axis(expert_pairs, placing[:, :, None], axis=1)
    return expert_pairs.reshape(TOKENS, 2).astype(jnp.int32)


def plant(result, own_key, least, top_value):
    dims = result.shape
    place = [jax.random.randint(jax.random.fold_in(own_key, axis), (), 0, dims[axis]) for axis in range(len(dims))]
    result = result.at[tuple(place)].set(least)
    longest = dims.index(max(dims))
    place[longest] = (place[longest] + 1) % dims[longest]
    return result.at[tuple(place)].set(top_value)


def block_scale(own_key, extent, pieces, low, high):
    def one(position, parts):
        heights = jax.random.uniform(jax.random.fold_in(jax.random.fold_in(own_key, 6), position), (parts,), jnp.float32, low / len(pieces), high / len(pieces))
        return jnp.repeat(jnp.exp(heights), extent[position] // parts).reshape((-1,) + (1,) * (len(extent) - position - 1))

    factor_of = one(*pieces[0])
    for cut in pieces[1:]:
        factor_of = factor_of * one(*cut)
    return factor_of


def scatter_about(rng, shape, width, bound, cuts=(), dtype=jnp.bfloat16):
    level = block_scale(rng, shape, cuts, -0.22, 0.18) if cuts else 1.0
    array = jax.random.normal(rng, shape, jnp.float32) * width * level
    return jnp.minimum(jnp.maximum(array, -bound), bound).astype(dtype)


def setup_inputs(seed: int = 0, part: int = 0) -> dict:
    keys = jax.random.split(jax.random.key(seed), 12)
    part_keys = jax.random.split(jax.random.fold_in(keys[11], part), 12)
    return {
        "tokens": scatter_about(part_keys[0], (TOKENS, D), 1.0, 6.0, ((0, 32),)),
        "expert_ids": draw_expert_ids(jax.random.fold_in(jax.random.fold_in(keys[11], part), 71), part),
        "gate_nums": plant(jax.random.randint(part_keys[2], (TOKENS, 2), 1, 9), jax.random.fold_in(part_keys[2], 1), 1, 8).astype(jnp.int32),
        "moe_gain": jnp.clip(1.0 + 0.18 * jax.random.normal(keys[3], (D,), jnp.float32), 0.1, 1.9),
        "w_gate_up": scatter_about(keys[4], (EXPERTS, D, 2, FF), D ** -0.5, 0.125, ((0, 4), (3, 8))),
        "w_down": scatter_about(keys[5], (EXPERTS, FF, D), FF ** -0.5, 0.09375, ((0, 4), (1, 8))),
        "attn_gain": jnp.clip(1.0 + 0.18 * jax.random.normal(keys[6], (D,), jnp.float32), 0.1, 1.9),
        "w_qkv": scatter_about(keys[7], (D, 3, HEADS * HD), D ** -0.5, 0.125, ((2, 8),)),
        "q_gain": jnp.clip(jax.random.uniform(keys[8], (HD,), jnp.float32, 1.2, 2.2), 1.2, 2.2),
        "k_gain": jnp.clip(jax.random.uniform(keys[9], (HD,), jnp.float32, 1.2, 2.2), 1.2, 2.2),
        "w_out": scatter_about(keys[10], (HEADS * HD, D), (HEADS * HD) ** -0.5, 0.125, ((0, 8),)),
    }


def rms_scale(values, gain):
    return values * lax.rsqrt(lax.optimization_barrier(jnp.mean(values * values, axis=-1, keepdims=True)) + 1e-06) * gain

def one_head(triple):
    queries, keys_all, values_all = triple
    scores = jnp.dot(queries, keys_all.T, preferred_element_type=jnp.float32) * (1.0 / math.sqrt(HD))
    probs = jnp.exp(scores)
    denom = lax.optimization_barrier(jnp.sum(probs, axis=1))
    numer = jnp.dot(probs.astype(jnp.bfloat16), values_all, preferred_element_type=jnp.float32)
    return (numer / denom[:, None]).astype(jnp.bfloat16)

def reference(tokens, expert_ids, gate_nums, moe_gain, w_gate_up, w_down, attn_gain, w_qkv, q_gain, k_gain, w_out):
    tokens_wide = tokens.astype(jnp.float32)
    normed = rms_scale(tokens_wide, moe_gain).astype(jnp.bfloat16)
    shard = FF // N_SEQ
    nums = gate_nums.astype(jnp.float32)
    weights = nums / lax.optimization_barrier(jnp.sum(nums, axis=1, keepdims=True))
    moe_total = jnp.zeros((TOKENS, D), jnp.float32)
    for expert in range(EXPERTS):
        gate_up = jnp.dot(normed, w_gate_up[expert].reshape(D, 2 * FF), preferred_element_type=jnp.float32).reshape(TOKENS, 2, FF)
        hidden = (jax.nn.silu(gate_up[:, 0]) * gate_up[:, 1]).astype(jnp.bfloat16)
        total = jnp.zeros((TOKENS, D), jnp.float32)
        for block in range(N_SEQ):
            partial_value = jnp.dot(hidden[:, block * shard:(block + 1) * shard], w_down[expert, block * shard:(block + 1) * shard], preferred_element_type=jnp.float32)
            total = total + lax.optimization_barrier(partial_value.astype(jnp.bfloat16)).astype(jnp.float32)
        share = lax.optimization_barrier(jnp.sum(jnp.where(expert_ids == expert, weights, jnp.zeros_like(weights)), axis=1))
        moe_total = moe_total + share[:, None] * total
    mixed = (tokens_wide + moe_total).astype(jnp.bfloat16)
    attn_in = rms_scale(mixed.astype(jnp.float32), attn_gain).astype(jnp.bfloat16)
    qkv = jnp.dot(attn_in, w_qkv.reshape(D, 3 * HEADS * HD), preferred_element_type=jnp.float32).reshape(TOKENS, 3, HEADS, HD)
    queries = rms_scale(qkv[:, 0], q_gain).astype(jnp.bfloat16)
    keys_all = rms_scale(qkv[:, 1], k_gain).astype(jnp.bfloat16)
    values_all = qkv[:, 2].astype(jnp.bfloat16)
    heads_out = lax.map(one_head, (queries.transpose(1, 0, 2), keys_all.transpose(1, 0, 2), values_all.transpose(1, 0, 2)))
    joined = heads_out.transpose(1, 0, 2).reshape(TOKENS, HEADS * HD)
    attended = (mixed.astype(jnp.float32) + jnp.dot(joined, w_out, preferred_element_type=jnp.float32)).astype(jnp.bfloat16)
    return (mixed, attended)
```

```python
import math

import jax
import jax.numpy as jnp
from jax import lax
from jax.experimental import pallas as pl
from jax.experimental.pallas import tpu as pltpu
from jax.sharding import Mesh
from jax.sharding import PartitionSpec as P

EXPERTS = 4
LANES = 128
EXP = ("exp_0", "exp_1")
SET_EXP_SEQ = ("set", "exp_0", "exp_1", "seq")


def swap(value, axis):
    return lax.ppermute(value, axis, [(0, 1), (1, 0)])


def shift(value, step):
    n = lax.axis_size("seq")
    return lax.ppermute(value, "seq", [(i, (i + step) % n) for i in range(n)])


def wide(value):
    return value.astype(jnp.float32)


def added(*values):
    total = wide(values[0])
    for v in values[1:]:
        total = total + wide(v)
    return total.astype(jnp.bfloat16)


def tied(first, second):
    return lax.optimization_barrier((first, second))


def rms_scale(values, gain):
    return values * lax.rsqrt(jnp.mean(values * values, axis=-1, keepdims=True) + 1e-06) * gain


def ring_scatter(far, below, above):
    rows = far[0].shape[0]
    half = rows // 2
    up = shift(added(*(t[:half] for t in far)), 1)
    down = shift(added(*(t[half:] for t in far)), -1)
    a3, b3 = above[2], below[2]
    acc_up = jnp.concatenate(
        [added(*(t[:half] for t in a3), up), added(*(t[half:] for t in a3))], 0
    )
    acc_down = jnp.concatenate(
        [added(*(t[:half] for t in b3)), added(*(t[half:] for t in b3), down)], 0
    )
    for r in (1, 0):
        up, down = shift(acc_up, 1), shift(acc_down, -1)
        acc_up, acc_down = added(*above[r], up), added(*below[r], down)
    return shift(acc_up, 1), shift(acc_down, -1)


ANY = pl.BlockSpec(memory_space=pl.ANY)


def expert_call(parts, w_gate, w_up, w_down, me):
    n = len(parts)
    rows = parts[0].shape[0]
    dim, ff = w_gate.shape
    m = n * rows
    kc = 512
    nk = dim // kc

    def kernel(me_ref, *refs):
        xs, (wg, wu, wd), outs = refs[:n], refs[n : n + 3], refs[n + 3 : 2 * n + 3]
        x_s, wg_s, wu_s, wd_s, ag, au, h_s, sh_s, sx, sg, su, sd = refs[2 * n + 3 :]

        def x_copy(i):
            return pltpu.make_async_copy(xs[i], x_s.at[pl.ds(i * rows, rows)], sx.at[i])

        def w_copy(w, w_s, sem, k):
            at = pl.ds(pl.multiple_of(k * kc, kc), kc)
            return pltpu.make_async_copy(w.at[at], w_s.at[at], sem.at[k])

        d_copy = pltpu.make_async_copy(wd, wd_s, sd)
        for i in range(n):
            x_copy(i).start()
        for k in range(nk):
            w_copy(wg, wg_s, sg, k).start()
            w_copy(wu, wu_s, su, k).start()
        d_copy.start()
        ag[...] = jnp.zeros_like(ag)
        au[...] = jnp.zeros_like(au)
        for i in range(n):
            x_copy(i).wait()
        nums = x_s[:, dim:].astype(jnp.float32)
        here = lax.broadcasted_iota(jnp.int32, nums.shape, 1) == me_ref[0]
        share = jnp.sum(jnp.where(here, nums, 0.0), axis=1, keepdims=True) / jnp.sum(
            nums, axis=1, keepdims=True
        )
        sh_s[...] = jnp.broadcast_to(share, sh_s.shape)

        def step(k, carry):
            at = pl.ds(pl.multiple_of(k * kc, kc), kc)
            w_copy(wg, wg_s, sg, k).wait()
            w_copy(wu, wu_s, su, k).wait()
            x = x_s[:, at]
            ag[...] += jnp.dot(x, wg_s[at, :], preferred_element_type=jnp.float32)
            au[...] += jnp.dot(x, wu_s[at, :], preferred_element_type=jnp.float32)
            return carry

        lax.fori_loop(0, nk, step, 0)
        gate = ag[...]
        h_s[...] = (gate / (1.0 + jnp.exp(-gate)) * au[...]).astype(jnp.bfloat16)
        d_copy.wait()

        def down(k, carry):
            at = pl.ds(pl.multiple_of(k * kc, kc), kc)
            y = jnp.dot(h_s[...], wd_s[:, at], preferred_element_type=jnp.float32)
            y = (y * sh_s[:, :1]).astype(jnp.bfloat16)
            for i in range(n):
                outs[i][:, at] = y[i * rows : (i + 1) * rows]
            return carry

        lax.fori_loop(0, nk, down, 0)

    return pl.pallas_call(
        kernel,
        out_shape=[jax.ShapeDtypeStruct((rows, dim), jnp.bfloat16)] * n,
        in_specs=[pl.BlockSpec(memory_space=pltpu.SMEM)] + [ANY] * (n + 3),
        out_specs=[pl.BlockSpec(memory_space=pltpu.VMEM)] * n,
        scratch_shapes=[
            pltpu.VMEM((m, parts[0].shape[1]), jnp.bfloat16),
            pltpu.VMEM((dim, ff), jnp.bfloat16),
            pltpu.VMEM((dim, ff), jnp.bfloat16),
            pltpu.VMEM((ff, dim), jnp.bfloat16),
            pltpu.VMEM((m, ff), jnp.float32),
            pltpu.VMEM((m, ff), jnp.float32),
            pltpu.VMEM((m, ff), jnp.bfloat16),
            pltpu.VMEM((m, LANES), jnp.float32),
            pltpu.SemaphoreType.DMA((n,)),
            pltpu.SemaphoreType.DMA((nk,)),
            pltpu.SemaphoreType.DMA((nk,)),
            pltpu.SemaphoreType.DMA,
        ],
        compiler_params=pltpu.CompilerParams(vmem_limit_bytes=24 * 2**20),
        cost_estimate=pl.CostEstimate(
            flops=6 * m * dim * ff, bytes_accessed=6 * dim * ff + 4 * m * dim, transcendentals=m * ff
        ),
        name="expert",
    )(me, *parts, w_gate, w_up, w_down)


def project_call(parts, w, q_gain, k_gain, heads):
    n = len(parts)
    sizes = [p.shape[0] for p in parts]
    m = sum(sizes)
    dim, cols = w.shape
    width = cols // 3
    head = width // heads
    kc = 512
    nk = dim // kc

    def kernel(*refs):
        xs, (w_ref, qg, kg, q_out, kv_out, x_s, w_s, acc, sx, sw) = refs[:n], refs[n:]

        def x_copy(i):
            return pltpu.make_async_copy(
                xs[i], x_s.at[pl.ds(sum(sizes[:i]), sizes[i])], sx.at[i]
            )

        def w_copy(k):
            at = pl.ds(pl.multiple_of(k * kc, kc), kc)
            return pltpu.make_async_copy(w_ref.at[at], w_s.at[at], sw.at[k])

        for i in range(n):
            x_copy(i).start()
        for k in range(nk):
            w_copy(k).start()
        acc[...] = jnp.zeros_like(acc)
        for i in range(n):
            x_copy(i).wait()

        def step(k, carry):
            at = pl.ds(pl.multiple_of(k * kc, kc), kc)
            w_copy(k).wait()
            acc[...] += jnp.dot(x_s[:, at], w_s[at, :], preferred_element_type=jnp.float32)
            return carry

        lax.fori_loop(0, nk, step, 0)
        for i in range(heads):
            at = slice(i * head, (i + 1) * head)
            q_out[:, at] = rms_scale(acc[:, at], qg[...]).astype(jnp.bfloat16)
            at_k = slice(width + i * head, width + (i + 1) * head)
            kv_out[:, at] = rms_scale(acc[:, at_k], kg[...]).astype(jnp.bfloat16)
        kv_out[:, width:] = acc[:, 2 * width :].astype(jnp.bfloat16)

    vmem = pl.BlockSpec(memory_space=pltpu.VMEM)
    return pl.pallas_call(
        kernel,
        out_shape=[
            jax.ShapeDtypeStruct((m, width), jnp.bfloat16),
            jax.ShapeDtypeStruct((m, 2 * width), jnp.bfloat16),
        ],
        in_specs=[ANY] * (n + 1) + [vmem, vmem],
        out_specs=[vmem, vmem],
        scratch_shapes=[
            pltpu.VMEM((m, dim), jnp.bfloat16),
            pltpu.VMEM((dim, cols), jnp.bfloat16),
            pltpu.VMEM((m, cols), jnp.float32),
            pltpu.SemaphoreType.DMA((n,)),
            pltpu.SemaphoreType.DMA((nk,)),
        ],
        compiler_params=pltpu.CompilerParams(vmem_limit_bytes=16 * 2**20),
        cost_estimate=pl.CostEstimate(
            flops=2 * m * dim * cols, bytes_accessed=2 * dim * cols + 2 * m * dim, transcendentals=0
        ),
        name="project",
    )(*parts, w, q_gain.reshape(1, -1), k_gain.reshape(1, -1))


def attend_call(queries, kvs, w_out, heads, rows):
    nq, nv = len(queries), len(kvs)
    m = sum(q.shape[0] for q in queries)
    t = sum(k.shape[0] for k in kvs)
    width = queries[0].shape[1]
    head = width // heads
    dim = w_out.shape[1]
    planes = m // rows
    scale_factor = 1.0 / math.sqrt(head)

    def kernel(*refs):
        qs, ks, w_ref = refs[:nq], refs[nq : nq + nv], refs[nq + nv]
        outs = refs[nq + nv + 1 : nq + nv + 1 + planes]
        q_s, kv_s, w_s, o_s, sq, sk, sw = refs[nq + nv + 1 + planes :]
        copies = []
        at = 0
        for i, k in enumerate(ks):
            copies.append(pltpu.make_async_copy(k, kv_s.at[pl.ds(at, k.shape[0])], sk.at[i]))
            at += k.shape[0]
        at = 0
        for i, q in enumerate(qs):
            copies.append(pltpu.make_async_copy(q, q_s.at[pl.ds(at, q.shape[0])], sq.at[i]))
            at += q.shape[0]
        w_copy = pltpu.make_async_copy(w_ref, w_s, sw)
        for c in copies:
            c.start()
        w_copy.start()
        for c in copies:
            c.wait()
        for i in range(heads):
            at = slice(i * head, (i + 1) * head)
            scores = (
                lax.dot_general(
                    q_s[:, at],
                    kv_s[:, at],
                    (((1,), (1,)), ((), ())),
                    preferred_element_type=jnp.float32,
                )
                * scale_factor
            )
            probs = jnp.exp(scores)
            denom = jnp.sum(probs, axis=1, keepdims=True)
            num = jnp.dot(
                probs.astype(jnp.bfloat16),
                kv_s[:, width + i * head : width + (i + 1) * head],
                preferred_element_type=jnp.float32,
            )
            o_s[:, at] = (num / denom).astype(jnp.bfloat16)
        w_copy.wait()
        kc = 512

        def out_step(k, carry):
            cols = pl.ds(pl.multiple_of(k * kc, kc), kc)
            y = jnp.dot(o_s[...], w_s[:, cols], preferred_element_type=jnp.float32)
            y = y.astype(jnp.bfloat16)
            for i in range(planes):
                outs[i][:, cols] = y[i * rows : (i + 1) * rows]
            return carry

        lax.fori_loop(0, dim // kc, out_step, 0)

    return pl.pallas_call(
        kernel,
        out_shape=[jax.ShapeDtypeStruct((rows, dim), jnp.bfloat16)] * planes,
        in_specs=[ANY] * (nq + nv + 1),
        out_specs=[pl.BlockSpec(memory_space=pltpu.VMEM)] * planes,
        scratch_shapes=[
            pltpu.VMEM((m, width), jnp.bfloat16),
            pltpu.VMEM((t, 2 * width), jnp.bfloat16),
            pltpu.VMEM(w_out.shape, jnp.bfloat16),
            pltpu.VMEM((m, width), jnp.bfloat16),
            pltpu.SemaphoreType.DMA((nq,)),
            pltpu.SemaphoreType.DMA((nv,)),
            pltpu.SemaphoreType.DMA,
        ],
        compiler_params=pltpu.CompilerParams(vmem_limit_bytes=32 * 2**20),
        cost_estimate=pl.CostEstimate(
            flops=4 * m * t * width + 2 * m * width * dim,
            bytes_accessed=2 * (t * 2 * width + width * dim + m * dim),
            transcendentals=m * t * heads,
        ),
        name="attend",
    )(*queries, *kvs, w_out)


def shards(
    tokens,
    expert_ids,
    gate_nums,
    moe_gain,
    w_gate_up,
    w_down,
    attn_gain,
    w_qkv,
    q_gain,
    k_gain,
    w_out,
):
    rows, dim = tokens.shape
    me = (lax.axis_index("exp_0") * 2 + lax.axis_index("exp_1")).reshape(1).astype(jnp.int32)
    w_down0 = w_down[0]

    tokens_wide = wide(tokens)
    normed = rms_scale(tokens_wide, moe_gain).astype(jnp.bfloat16)
    lane = lax.broadcasted_iota(jnp.int32, (rows, LANES), 1)
    numer = jnp.where(expert_ids[:, :1] == lane, gate_nums[:, :1], 0) + jnp.where(
        expert_ids[:, 1:] == lane, gate_nums[:, 1:], 0
    )
    packed = jnp.concatenate([normed, numer.astype(jnp.bfloat16)], axis=1)

    beside = swap(packed, "exp_0")
    w_gate, w_up, beside = lax.optimization_barrier(
        (w_gate_up[0, :, 0, :], w_gate_up[0, :, 1, :], beside)
    )
    column = jnp.concatenate([packed, beside], 0)
    up, down = shift(column, 1), shift(column, -1)
    w_qkv2 = w_qkv.reshape(dim, -1)

    def experts(parts):
        n = len(parts)
        out = expert_call([*parts, *(swap(p, "exp_1") for p in parts)], w_gate, w_up, w_down0, me)
        return [(out[i], swap(out[n + i], "exp_1")) for i in range(n)]

    (own_terms,) = experts([column])
    below, above = [], []
    (up, down), (own_terms, w_qkv2) = tied((up, down), (own_terms, w_qkv2))
    half = column.shape[0] // 2
    for r in range(3):
        step = column.shape[0] if r < 2 else half
        here = (up, down)
        up, down = shift(up[:step], 1), shift(down[-step:], -1)
        lo, hi = experts(here)
        (up, down), (lo, hi) = tied((up, down), (lo, hi))
        below.append(lo)
        above.append(hi)
    far_terms = experts([up, down])
    far_terms = [jnp.concatenate([a, b], 0) for a, b in zip(*far_terms)]
    from_below, from_above = ring_scatter(far_terms, below, above)
    total = wide(own_terms[0]) + wide(own_terms[1]) + wide(from_below) + wide(from_above)
    moe_total = total[:rows] + wide(swap(total[rows:].astype(jnp.bfloat16), "exp_0"))
    mixed = (tokens_wide + moe_total).astype(jnp.bfloat16)

    mixed_wide = wide(mixed)
    attn_in = rms_scale(mixed_wide, attn_gain).astype(jnp.bfloat16)
    head = q_gain.shape[0]
    heads = w_qkv.shape[2] // head

    def project(parts):
        q, kv = project_call(parts, w_qkv2, q_gain, k_gain, heads)
        beside = swap(kv, "exp_0")
        return q, [kv, beside, swap(kv, "exp_1"), swap(beside, "exp_1")]

    half = rows // 2
    up1, down1 = shift(attn_in, 1), shift(attn_in, -1)
    up2, down2 = shift(up1, 1), shift(down1, -1)
    q_a, kv_a = project([attn_in, up1, down1])
    (up2, down2), (q_a, kv_a) = tied((up2, down2), (q_a, kv_a))
    up3, down3 = shift(up2, 1), shift(down2, -1)
    far = (shift(up3[:half], 1), shift(down3[half:], -1))
    q_b, kv_b = project([up2, down2, up3, down3])
    far, (q_b, kv_b) = tied(far, (q_b, kv_b))
    q_c, kv_c = project([jnp.concatenate(far, 0)])
    piece = attend_call([q_a, q_b, q_c], kv_a + kv_b + kv_c, w_out, heads, rows)
    from_below, from_above = ring_scatter(
        (piece[7],), [(p,) for p in piece[1:7:2]], [(p,) for p in piece[2:7:2]]
    )
    attended = (
        mixed_wide + (wide(piece[0]) + wide(from_below) + wide(from_above))
    ).astype(jnp.bfloat16)
    return (mixed, attended)


def solution(mesh):
    torus = Mesh(
        mesh.devices.reshape(mesh.shape["set"], 2, 2, mesh.shape["seq"]),
        ("set", "exp_0", "exp_1", "seq"),
    )
    in_specs = (
        P(SET_EXP_SEQ, None),
        P(SET_EXP_SEQ, None),
        P(SET_EXP_SEQ, None),
        P(),
        P(EXP, None, None, "seq"),
        P(EXP, "seq", None),
        P(),
        P(None, None, "seq"),
        P(),
        P(),
        P("seq", None),
    )
    out_specs = (P(SET_EXP_SEQ, None), P(SET_EXP_SEQ, None))
    return jax.shard_map(
        shards, mesh=torus, in_specs=in_specs, out_specs=out_specs, check_vma=False
    )
```

```python
import math

import jax
import jax.numpy as jnp
from jax import lax
from jax.experimental import pallas as pl
from jax.experimental.pallas import tpu as pltpu
from jax.sharding import Mesh
from jax.sharding import PartitionSpec as P


LANES = 128
EXP = ("exp_0", "exp_1")
SET_EXP_SEQ = ("set", "exp_0", "exp_1", "seq")


def swap(value, axis):
    return lax.ppermute(value, axis, [(0, 1), (1, 0)])


def shift(value, step):
    n = lax.axis_size("seq")
    return lax.ppermute(value, "seq", [(i, (i + step) % n) for i in range(n)])


def wide(value):
    return value.astype(jnp.float32)


def added(*values):
    total = wide(values[0])
    for v in values[1:]:
        total = total + wide(v)
    return total.astype(jnp.bfloat16)


def tied(first, second):
    return lax.optimization_barrier((first, second))


def rms_scale(values, gain):
    return values * lax.rsqrt(jnp.mean(values * values, axis=-1, keepdims=True) + 1e-06) * gain


def ring_scatter(far, above, below):
    rows = far.shape[0]
    half = rows // 2
    blank = jnp.zeros((half, far.shape[1]), jnp.bfloat16)
    up = jnp.concatenate([shift(far[:half], 1), blank], 0)
    down = jnp.concatenate([blank, shift(far[half:], -1)], 0)

    def step(i, carry):
        up, down = carry
        at_up = lax.dynamic_slice_in_dim(above, i * rows, rows)
        at_down = lax.dynamic_slice_in_dim(below, i * rows, rows)
        return shift(added(at_up, up), 1), shift(added(at_down, down), -1)

    return lax.fori_loop(0, 3, step, (up, down))


ANY = pl.BlockSpec(memory_space=pl.ANY)


TRANS = (((1,), (1,)), ((), ()))


def expert_call(mine, other, w_gate, w_up, w_down, me):
    n = len(mine)
    plane = mine[0].shape[0]
    half = plane // 2
    ff, dim = w_gate.shape
    cols = mine[0].shape[1]
    m1 = n * plane
    m = 2 * m1
    kc = 512
    nk = dim // kc

    def kernel(me_ref, *refs):
        xs, (ox, wg, wu, wd, out_mine, out_other) = refs[:n], refs[n : n + 6]
        x_s, wg_s, wu_s, wd_s, ag, au, h_s, sh_s, sx, sg, su, sd = refs[n + 6 :]

        def w_copy(w, w_s, sem, k):
            at = pl.ds(pl.multiple_of(k * kc, kc), kc)
            return pltpu.make_async_copy(w.at[:, at], w_s.at[:, at], sem.at[k])

        copies = []
        for i in range(n):
            for b in range(2):
                src = pl.ds(b * half, half)
                dst = (b * n + i) * half
                copies.append(
                    pltpu.make_async_copy(
                        xs[i].at[src], x_s.at[pl.ds(dst, half)], sx.at[0, 2 * i + b]
                    )
                )
                src = pl.ds(i * plane + b * half, half)
                copies.append(
                    pltpu.make_async_copy(
                        ox.at[src], x_s.at[pl.ds(m1 + dst, half)], sx.at[1, 2 * i + b]
                    )
                )
        d_copy = pltpu.make_async_copy(wd, wd_s, sd)
        for c in copies:
            c.start()
        for k in range(nk):
            w_copy(wg, wg_s, sg, k).start()
            w_copy(wu, wu_s, su, k).start()
        d_copy.start()
        ag[...] = jnp.zeros_like(ag)
        au[...] = jnp.zeros_like(au)
        for c in copies:
            c.wait()
        nums = x_s[:, dim:].astype(jnp.float32)
        here = lax.broadcasted_iota(jnp.int32, nums.shape, 1) == me_ref[0]
        share = jnp.sum(jnp.where(here, nums, 0.0), axis=1, keepdims=True) / jnp.sum(
            nums, axis=1, keepdims=True
        )
        sh_s[...] = jnp.broadcast_to(share, sh_s.shape)

        def step(k, carry):
            at = pl.ds(pl.multiple_of(k * kc, kc), kc)
            w_copy(wg, wg_s, sg, k).wait()
            w_copy(wu, wu_s, su, k).wait()
            x = x_s[:, at]
            ag[...] += lax.dot_general(x, wg_s[:, at], TRANS, preferred_element_type=jnp.float32)
            au[...] += lax.dot_general(x, wu_s[:, at], TRANS, preferred_element_type=jnp.float32)
            return carry

        lax.fori_loop(0, nk, step, 0)
        gate = ag[...]
        h_s[...] = (gate / (1.0 + jnp.exp(-gate)) * au[...]).astype(jnp.bfloat16)
        d_copy.wait()

        def down(k, carry):
            at = pl.ds(pl.multiple_of(k * kc, kc), kc)
            y = jnp.dot(h_s[...], wd_s[:, at], preferred_element_type=jnp.float32)
            y = (y * sh_s[:, :1]).astype(jnp.bfloat16)
            out_mine[:, at] = y[:m1]
            out_other[:, at] = y[m1:]
            return carry

        lax.fori_loop(0, nk, down, 0)

    return pl.pallas_call(
        kernel,
        out_shape=[jax.ShapeDtypeStruct((m1, dim), jnp.bfloat16)] * 2,
        in_specs=[pl.BlockSpec(memory_space=pltpu.SMEM)] + [ANY] * (n + 4),
        out_specs=[pl.BlockSpec(memory_space=pltpu.VMEM)] * 2,
        scratch_shapes=[
            pltpu.VMEM((m, cols), jnp.bfloat16),
            pltpu.VMEM((ff, dim), jnp.bfloat16),
            pltpu.VMEM((ff, dim), jnp.bfloat16),
            pltpu.VMEM((ff, dim), jnp.bfloat16),
            pltpu.VMEM((m, ff), jnp.float32),
            pltpu.VMEM((m, ff), jnp.float32),
            pltpu.VMEM((m, ff), jnp.bfloat16),
            pltpu.VMEM((m, LANES), jnp.float32),
            pltpu.SemaphoreType.DMA((2, 2 * n)),
            pltpu.SemaphoreType.DMA((nk,)),
            pltpu.SemaphoreType.DMA((nk,)),
            pltpu.SemaphoreType.DMA,
        ],
        compiler_params=pltpu.CompilerParams(vmem_limit_bytes=28 * 2**20),
        cost_estimate=pl.CostEstimate(
            flops=6 * m * dim * ff, bytes_accessed=6 * dim * ff + 4 * m * dim, transcendentals=m * ff
        ),
        name="expert",
    )(me, *mine, other, w_gate, w_up, w_down)


def project_call(parts, w, q_gain, k_gain, heads):
    n = len(parts)
    sizes = [p.shape[0] for p in parts]
    m = sum(sizes)
    cols, dim = w.shape
    width = cols // 3
    head = width // heads
    kc = 512
    nk = dim // kc

    def kernel(*refs):
        xs, (w_ref, qg, kg, q_out, kv_out, x_s, w_s, acc, sx, sw) = refs[:n], refs[n:]

        def x_copy(i):
            return pltpu.make_async_copy(
                xs[i], x_s.at[pl.ds(sum(sizes[:i]), sizes[i])], sx.at[i]
            )

        def w_copy(k):
            at = pl.ds(pl.multiple_of(k * kc, kc), kc)
            return pltpu.make_async_copy(w_ref.at[:, at], w_s.at[:, at], sw.at[k])

        for i in range(n):
            x_copy(i).start()
        for k in range(nk):
            w_copy(k).start()
        acc[...] = jnp.zeros_like(acc)
        for i in range(n):
            x_copy(i).wait()

        def step(k, carry):
            at = pl.ds(pl.multiple_of(k * kc, kc), kc)
            w_copy(k).wait()
            acc[...] += lax.dot_general(
                x_s[:, at], w_s[:, at], TRANS, preferred_element_type=jnp.float32
            )
            return carry

        lax.fori_loop(0, nk, step, 0)
        for i in range(heads):
            at = slice(i * head, (i + 1) * head)
            q_out[:, at] = rms_scale(acc[:, at], qg[...]).astype(jnp.bfloat16)
            at_k = slice(width + i * head, width + (i + 1) * head)
            kv_out[:, at] = rms_scale(acc[:, at_k], kg[...]).astype(jnp.bfloat16)
        kv_out[:, width:] = acc[:, 2 * width :].astype(jnp.bfloat16)

    vmem = pl.BlockSpec(memory_space=pltpu.VMEM)
    return pl.pallas_call(
        kernel,
        out_shape=[
            jax.ShapeDtypeStruct((m, width), jnp.bfloat16),
            jax.ShapeDtypeStruct((m, 2 * width), jnp.bfloat16),
        ],
        in_specs=[ANY] * (n + 1) + [vmem, vmem],
        out_specs=[vmem, vmem],
        scratch_shapes=[
            pltpu.VMEM((m, dim), jnp.bfloat16),
            pltpu.VMEM((cols, dim), jnp.bfloat16),
            pltpu.VMEM((m, cols), jnp.float32),
            pltpu.SemaphoreType.DMA((n,)),
            pltpu.SemaphoreType.DMA((nk,)),
        ],
        compiler_params=pltpu.CompilerParams(vmem_limit_bytes=16 * 2**20),
        cost_estimate=pl.CostEstimate(
            flops=2 * m * dim * cols, bytes_accessed=2 * dim * cols + 2 * m * dim, transcendentals=0
        ),
        name="project",
    )(*parts, w, q_gain.reshape(1, -1), k_gain.reshape(1, -1))


def attend_call(queries, kvs, w_out, heads, rows):
    nq, nv = len(queries), len(kvs)
    m = sum(q.shape[0] for q in queries)
    t = sum(k.shape[0] for k in kvs)
    width = queries[0].shape[1]
    head = width // heads
    dim = w_out.shape[1]
    planes = m // rows
    scale_factor = 1.0 / math.sqrt(head)

    def kernel(*refs):
        qs, ks, w_ref = refs[:nq], refs[nq : nq + nv], refs[nq + nv]
        outs = refs[nq + nv + 1 : nq + nv + 1 + planes]
        q_s, kv_s, w_s, o_s, sq, sk, sw = refs[nq + nv + 1 + planes :]
        copies = []
        at = 0
        for i, k in enumerate(ks):
            copies.append(pltpu.make_async_copy(k, kv_s.at[pl.ds(at, k.shape[0])], sk.at[i]))
            at += k.shape[0]
        at = 0
        for i, q in enumerate(qs):
            copies.append(pltpu.make_async_copy(q, q_s.at[pl.ds(at, q.shape[0])], sq.at[i]))
            at += q.shape[0]
        w_copy = pltpu.make_async_copy(w_ref, w_s, sw)
        for c in copies:
            c.start()
        w_copy.start()
        for c in copies:
            c.wait()
        for i in range(heads):
            at = slice(i * head, (i + 1) * head)
            scores = (
                lax.dot_general(
                    q_s[:, at],
                    kv_s[:, at],
                    (((1,), (1,)), ((), ())),
                    preferred_element_type=jnp.float32,
                )
                * scale_factor
            )
            probs = jnp.exp(scores)
            denom = jnp.sum(probs, axis=1, keepdims=True)
            num = jnp.dot(
                probs.astype(jnp.bfloat16),
                kv_s[:, width + i * head : width + (i + 1) * head],
                preferred_element_type=jnp.float32,
            )
            o_s[:, at] = (num / denom).astype(jnp.bfloat16)
        w_copy.wait()
        kc = 512

        def out_step(k, carry):
            cols = pl.ds(pl.multiple_of(k * kc, kc), kc)
            y = jnp.dot(o_s[...], w_s[:, cols], preferred_element_type=jnp.float32)
            y = y.astype(jnp.bfloat16)
            for i in range(planes):
                outs[i][:, cols] = y[i * rows : (i + 1) * rows]
            return carry

        lax.fori_loop(0, dim // kc, out_step, 0)

    return pl.pallas_call(
        kernel,
        out_shape=[jax.ShapeDtypeStruct((rows, dim), jnp.bfloat16)] * planes,
        in_specs=[ANY] * (nq + nv + 1),
        out_specs=[pl.BlockSpec(memory_space=pltpu.VMEM)] * planes,
        scratch_shapes=[
            pltpu.VMEM((m, width), jnp.bfloat16),
            pltpu.VMEM((t, 2 * width), jnp.bfloat16),
            pltpu.VMEM(w_out.shape, jnp.bfloat16),
            pltpu.VMEM((m, width), jnp.bfloat16),
            pltpu.SemaphoreType.DMA((nq,)),
            pltpu.SemaphoreType.DMA((nv,)),
            pltpu.SemaphoreType.DMA,
        ],
        compiler_params=pltpu.CompilerParams(vmem_limit_bytes=32 * 2**20),
        cost_estimate=pl.CostEstimate(
            flops=4 * m * t * width + 2 * m * width * dim,
            bytes_accessed=2 * (t * 2 * width + width * dim + m * dim),
            transcendentals=m * t * heads,
        ),
        name="attend",
    )(*queries, *kvs, w_out)


def shards(
    tokens,
    expert_ids,
    gate_nums,
    moe_gain,
    w_gate_up,
    w_down,
    attn_gain,
    w_qkv,
    q_gain,
    k_gain,
    w_out,
):
    rows, dim = tokens.shape
    me = (lax.axis_index("exp_0") * 2 + lax.axis_index("exp_1")).reshape(1).astype(jnp.int32)
    w_down0 = w_down[0]

    tokens_wide = wide(tokens)
    normed = rms_scale(tokens_wide, moe_gain).astype(jnp.bfloat16)
    lane = lax.broadcasted_iota(jnp.int32, (rows, LANES), 1)
    numer = jnp.where(expert_ids[:, :1] == lane, gate_nums[:, :1], 0) + jnp.where(
        expert_ids[:, 1:] == lane, gate_nums[:, 1:], 0
    )
    packed = jnp.concatenate([normed, numer.astype(jnp.bfloat16)], axis=1)

    column = jnp.concatenate([packed, swap(packed, "exp_0")], 0)
    w_gate = w_gate_up[0, :, 0, :].T
    w_up = w_gate_up[0, :, 1, :].T

    def experts(planes):
        other = swap(jnp.concatenate(planes, 0) if len(planes) > 1 else planes[0], "exp_1")
        mine, theirs = expert_call(planes, other, w_gate, w_up, w_down0, me)
        chip = added(mine, swap(theirs, "exp_1"))
        cut = rows * len(planes)
        across = swap(chip[cut:], "exp_0")
        return [
            (chip[i * rows : (i + 1) * rows], across[i * rows : (i + 1) * rows])
            for i in range(len(planes))
        ]

    up1, down1 = shift(column, 1), shift(column, -1)
    up2, down2 = shift(up1, 1), shift(down1, -1)
    own_terms, b1, a1 = experts([column, up1, down1])
    up3, down3 = shift(up2, 1), shift(down2, -1)
    b2, a2 = experts([up2, down2])
    far_up, far_down = shift(up3[:rows], 1), shift(down3[rows:], -1)
    b3, a3 = experts([up3, down3])
    (far_terms,) = experts([jnp.concatenate([far_up, far_down], 0)])
    far_sum, w_qkv0 = tied(added(*far_terms), w_qkv)
    w_qkv2 = w_qkv0.transpose(1, 2, 0).reshape(-1, dim)
    above = jnp.concatenate([added(*a3), added(*a2), added(*a1)], 0)
    below = jnp.concatenate([added(*b3), added(*b2), added(*b1)], 0)
    from_below, from_above = ring_scatter(far_sum, above, below)
    (from_below, from_above), w_qkv2 = tied((from_below, from_above), w_qkv2)
    moe_total = wide(own_terms[0]) + wide(own_terms[1]) + wide(from_below) + wide(from_above)
    mixed = (tokens_wide + moe_total).astype(jnp.bfloat16)

    mixed_wide = wide(mixed)
    attn_in = rms_scale(mixed_wide, attn_gain).astype(jnp.bfloat16)
    head = q_gain.shape[0]
    heads = w_qkv.shape[2] // head

    def project(parts):
        q, kv = project_call(parts, w_qkv2, q_gain, k_gain, heads)
        return q, lax.all_gather(kv, EXP, axis=0, tiled=True)

    half = rows // 2
    up1, down1 = shift(attn_in, 1), shift(attn_in, -1)
    up2, down2 = shift(up1, 1), shift(down1, -1)
    q_a, kv_a = project([attn_in, up1, down1])
    up3, down3 = shift(up2, 1), shift(down2, -1)
    far = (shift(up3[:half], 1), shift(down3[half:], -1))
    q_b, kv_b = project([up2, down2, up3, down3])
    q_c, kv_c = project([jnp.concatenate(far, 0)])
    piece = attend_call([q_a, q_b, q_c], [kv_a, kv_b, kv_c], w_out, heads, rows)
    from_below, from_above = ring_scatter(
        piece[7], jnp.concatenate(piece[6:1:-2], 0), jnp.concatenate(piece[5:0:-2], 0)
    )
    attended = (
        mixed_wide + (wide(piece[0]) + wide(from_below) + wide(from_above))
    ).astype(jnp.bfloat16)
    return (mixed, attended)


def solution(mesh):
    torus = Mesh(
        mesh.devices.reshape(mesh.shape["set"], 2, 2, mesh.shape["seq"]),
        ("set", "exp_0", "exp_1", "seq"),
    )
    in_specs = (
        P(SET_EXP_SEQ, None),
        P(SET_EXP_SEQ, None),
        P(SET_EXP_SEQ, None),
        P(),
        P(EXP, None, None, "seq"),
        P(EXP, "seq", None),
        P(),
        P(None, None, "seq"),
        P(),
        P(),
        P("seq", None),
    )
    out_specs = (P(SET_EXP_SEQ, None), P(SET_EXP_SEQ, None))

    return jax.shard_map(shards, mesh=torus, in_specs=in_specs, out_specs=out_specs, check_vma=False)
```

```python
import math

import jax
import jax.numpy as jnp
from jax import lax
from jax.experimental import pallas as pl
from jax.experimental.pallas import tpu as pltpu
from jax.sharding import Mesh
from jax.sharding import PartitionSpec as P


LANES = 128
EXP = ("exp_0", "exp_1")
SET_EXP_SEQ = ("set", "exp_0", "exp_1", "seq")


def swap(value, axis):
    return lax.ppermute(value, axis, [(0, 1), (1, 0)])


def shift(value, step):
    n = lax.axis_size("seq")
    return lax.ppermute(value, "seq", [(i, (i + step) % n) for i in range(n)])


def wide(value):
    return value.astype(jnp.float32)


def added(*values):
    total = wide(values[0])
    for v in values[1:]:
        total = total + wide(v)
    return total.astype(jnp.bfloat16)


def tied(first, second):
    return lax.optimization_barrier((first, second))


def rms_scale(values, gain):
    return values * lax.rsqrt(jnp.mean(values * values, axis=-1, keepdims=True) + 1e-06) * gain


def ring_scatter(above, below, rows):
    blank = jnp.zeros((rows, above.shape[1]), jnp.bfloat16)

    def step(i, carry):
        up, down = carry
        at_up = lax.dynamic_slice_in_dim(above, i * rows, rows)
        at_down = lax.dynamic_slice_in_dim(below, i * rows, rows)
        return shift(added(at_up, up), 1), shift(added(at_down, down), -1)

    return lax.fori_loop(0, above.shape[0] // rows, step, (blank, blank))


ANY = pl.BlockSpec(memory_space=pl.ANY)


TRANS = (((1,), (1,)), ((), ()))


def expert_call(mine, other, w_gate_up, w_down, me):
    n = len(mine)
    plane = mine[0].shape[0]
    half = plane // 2
    _, fb, dim = w_gate_up.shape
    ff = 2 * fb
    cols = mine[0].shape[1]
    m1 = n * plane
    m = 2 * m1
    kc = 512
    nk = dim // kc

    def kernel(me_ref, *refs):
        xs, (ox, wgu, wd, out_mine, out_other) = refs[:n], refs[n : n + 5]
        x_s, wgu_s, wd_s, acc, h_s, sh_s, sx, sg, sd = refs[n + 5 :]

        def w_copy(k):
            return pltpu.make_async_copy(wgu.at[k], wgu_s.at[k], sg.at[k])

        copies = []
        for i in range(n):
            for b in range(2):
                src = pl.ds(b * half, half)
                dst = (b * n + i) * half
                copies.append(
                    pltpu.make_async_copy(
                        xs[i].at[src], x_s.at[pl.ds(dst, half)], sx.at[0, 2 * i + b]
                    )
                )
                src = pl.ds(i * plane + b * half, half)
                copies.append(
                    pltpu.make_async_copy(
                        ox.at[src], x_s.at[pl.ds(m1 + dst, half)], sx.at[1, 2 * i + b]
                    )
                )
        d_copy = pltpu.make_async_copy(wd, wd_s, sd)
        for c in copies:
            c.start()
        for k in range(4):
            w_copy(k).start()
        d_copy.start()
        for c in copies:
            c.wait()
        nums = x_s[:, dim:].astype(jnp.float32)
        here = lax.broadcasted_iota(jnp.int32, nums.shape, 1) == me_ref[0]
        share = jnp.sum(jnp.where(here, nums, 0.0), axis=1, keepdims=True) / jnp.sum(
            nums, axis=1, keepdims=True
        )
        sh_s[...] = jnp.broadcast_to(share, sh_s.shape)

        def step(k, carry):
            w_copy(k).wait()
            acc[k] = lax.dot_general(
                x_s[:, :dim], wgu_s[k], TRANS, preferred_element_type=jnp.float32
            )
            return carry

        lax.fori_loop(0, 4, step, 0)
        for b in range(2):
            gate = acc[b]
            h_s[b] = (gate / (1.0 + jnp.exp(-gate)) * acc[2 + b]).astype(jnp.bfloat16)
        d_copy.wait()

        def down(k, carry):
            at = pl.ds(pl.multiple_of(k * kc, kc), kc)
            y = jnp.dot(h_s[0], wd_s[0, :, at], preferred_element_type=jnp.float32) + jnp.dot(
                h_s[1], wd_s[1, :, at], preferred_element_type=jnp.float32
            )
            y = (y * sh_s[:, :1]).astype(jnp.bfloat16)
            out_mine[:, at] = y[:m1]
            out_other[:, at] = y[m1:]
            return carry

        lax.fori_loop(0, nk, down, 0)

    return pl.pallas_call(
        kernel,
        out_shape=[jax.ShapeDtypeStruct((m1, dim), jnp.bfloat16)] * 2,
        in_specs=[pl.BlockSpec(memory_space=pltpu.SMEM)] + [ANY] * (n + 3),
        out_specs=[pl.BlockSpec(memory_space=pltpu.VMEM)] * 2,
        scratch_shapes=[
            pltpu.VMEM((m, cols), jnp.bfloat16),
            pltpu.VMEM((4, fb, dim), jnp.bfloat16),
            pltpu.VMEM((2, fb, dim), jnp.bfloat16),
            pltpu.VMEM((4, m, fb), jnp.float32),
            pltpu.VMEM((2, m, fb), jnp.bfloat16),
            pltpu.VMEM((m, LANES), jnp.float32),
            pltpu.SemaphoreType.DMA((2, 2 * n)),
            pltpu.SemaphoreType.DMA((4,)),
            pltpu.SemaphoreType.DMA,
        ],
        compiler_params=pltpu.CompilerParams(vmem_limit_bytes=(10 + 5 * n) * 2**20),
        cost_estimate=pl.CostEstimate(
            flops=6 * m * dim * ff, bytes_accessed=6 * dim * ff + 4 * m * dim, transcendentals=m * ff
        ),
        name="expert",
    )(me, *mine, other, w_gate_up, w_down)


def project_call(parts, w, q_gain, k_gain, heads):
    n = len(parts)
    sizes = [p.shape[0] for p in parts]
    m = sum(sizes)
    cols, dim = w.shape
    width = cols // 3
    head = width // heads
    kc = 512
    nk = dim // kc

    def kernel(*refs):
        xs, (w_ref, qg, kg, q_out, kv_out, x_s, w_s, acc, sx, sw) = refs[:n], refs[n:]

        def x_copy(i):
            return pltpu.make_async_copy(
                xs[i], x_s.at[pl.ds(sum(sizes[:i]), sizes[i])], sx.at[i]
            )

        def w_copy(k):
            at = pl.ds(pl.multiple_of(k * kc, kc), kc)
            return pltpu.make_async_copy(w_ref.at[:, at], w_s.at[:, at], sw.at[k])

        for i in range(n):
            x_copy(i).start()
        for k in range(nk):
            w_copy(k).start()
        acc[...] = jnp.zeros_like(acc)
        for i in range(n):
            x_copy(i).wait()

        def step(k, carry):
            at = pl.ds(pl.multiple_of(k * kc, kc), kc)
            w_copy(k).wait()
            acc[...] += lax.dot_general(
                x_s[:, at], w_s[:, at], TRANS, preferred_element_type=jnp.float32
            )
            return carry

        lax.fori_loop(0, nk, step, 0)
        for i in range(heads):
            at = slice(i * head, (i + 1) * head)
            q_out[:, at] = rms_scale(acc[:, at], qg[...]).astype(jnp.bfloat16)
            at_k = slice(width + i * head, width + (i + 1) * head)
            kv_out[:, at] = rms_scale(acc[:, at_k], kg[...]).astype(jnp.bfloat16)
        kv_out[:, width:] = acc[:, 2 * width :].astype(jnp.bfloat16)

    vmem = pl.BlockSpec(memory_space=pltpu.VMEM)
    return pl.pallas_call(
        kernel,
        out_shape=[
            jax.ShapeDtypeStruct((m, width), jnp.bfloat16),
            jax.ShapeDtypeStruct((m, 2 * width), jnp.bfloat16),
        ],
        in_specs=[ANY] * (n + 1) + [vmem, vmem],
        out_specs=[vmem, vmem],
        scratch_shapes=[
            pltpu.VMEM((m, dim), jnp.bfloat16),
            pltpu.VMEM((cols, dim), jnp.bfloat16),
            pltpu.VMEM((m, cols), jnp.float32),
            pltpu.SemaphoreType.DMA((n,)),
            pltpu.SemaphoreType.DMA((nk,)),
        ],
        compiler_params=pltpu.CompilerParams(vmem_limit_bytes=16 * 2**20),
        cost_estimate=pl.CostEstimate(
            flops=2 * m * dim * cols, bytes_accessed=2 * dim * cols + 2 * m * dim, transcendentals=0
        ),
        name="project",
    )(*parts, w, q_gain.reshape(1, -1), k_gain.reshape(1, -1))


def attend_call(queries, kvs, w_out, heads, rows):
    nq, nv = len(queries), len(kvs)
    m = sum(q.shape[0] for q in queries)
    t = sum(k.shape[0] for k in kvs)
    width = queries[0].shape[1]
    head = width // heads
    dim = w_out.shape[1]
    planes = m // rows
    scale_factor = 1.0 / math.sqrt(head)

    def kernel(*refs):
        qs, ks, w_ref = refs[:nq], refs[nq : nq + nv], refs[nq + nv]
        outs = refs[nq + nv + 1 : nq + nv + 1 + planes]
        q_s, kv_s, w_s, o_s, sq, sk, sw = refs[nq + nv + 1 + planes :]
        copies = []
        at = 0
        for i, k in enumerate(ks):
            copies.append(pltpu.make_async_copy(k, kv_s.at[pl.ds(at, k.shape[0])], sk.at[i]))
            at += k.shape[0]
        at = 0
        for i, q in enumerate(qs):
            copies.append(pltpu.make_async_copy(q, q_s.at[pl.ds(at, q.shape[0])], sq.at[i]))
            at += q.shape[0]
        w_copy = pltpu.make_async_copy(w_ref, w_s, sw)
        for c in copies:
            c.start()
        w_copy.start()
        for c in copies:
            c.wait()
        block = 128

        def rows_step(b, carry):
            r = pl.ds(pl.multiple_of(b * block, block), block)
            for i in range(heads):
                at = slice(i * head, (i + 1) * head)
                scores = (
                    lax.dot_general(
                        q_s[r, at], kv_s[:, at], TRANS, preferred_element_type=jnp.float32
                    )
                    * scale_factor
                )
                probs = jnp.exp(scores)
                denom = jnp.sum(probs, axis=1, keepdims=True)
                num = jnp.dot(
                    probs.astype(jnp.bfloat16),
                    kv_s[:, width + i * head : width + (i + 1) * head],
                    preferred_element_type=jnp.float32,
                )
                o_s[r, at] = (num / denom).astype(jnp.bfloat16)
            return carry

        lax.fori_loop(0, m // block, rows_step, 0)
        w_copy.wait()
        kc = 512

        def out_step(k, carry):
            cols = pl.ds(pl.multiple_of(k * kc, kc), kc)
            y = jnp.dot(o_s[...], w_s[:, cols], preferred_element_type=jnp.float32)
            y = y.astype(jnp.bfloat16)
            for i in range(planes):
                outs[i][:, cols] = y[i * rows : (i + 1) * rows]
            return carry

        lax.fori_loop(0, dim // kc, out_step, 0)

    return pl.pallas_call(
        kernel,
        out_shape=[jax.ShapeDtypeStruct((rows, dim), jnp.bfloat16)] * planes,
        in_specs=[ANY] * (nq + nv + 1),
        out_specs=[pl.BlockSpec(memory_space=pltpu.VMEM)] * planes,
        scratch_shapes=[
            pltpu.VMEM((m, width), jnp.bfloat16),
            pltpu.VMEM((t, 2 * width), jnp.bfloat16),
            pltpu.VMEM(w_out.shape, jnp.bfloat16),
            pltpu.VMEM((m, width), jnp.bfloat16),
            pltpu.SemaphoreType.DMA((nq,)),
            pltpu.SemaphoreType.DMA((nv,)),
            pltpu.SemaphoreType.DMA,
        ],
        compiler_params=pltpu.CompilerParams(vmem_limit_bytes=32 * 2**20),
        cost_estimate=pl.CostEstimate(
            flops=4 * m * t * width + 2 * m * width * dim,
            bytes_accessed=2 * (t * 2 * width + width * dim + m * dim),
            transcendentals=m * t * heads,
        ),
        name="attend",
    )(*queries, *kvs, w_out)


def shards(
    tokens,
    expert_ids,
    gate_nums,
    moe_gain,
    w_gate_up,
    w_down,
    attn_gain,
    w_qkv,
    q_gain,
    k_gain,
    w_out,
):
    rows, dim = tokens.shape
    me = (lax.axis_index("exp_0") * 2 + lax.axis_index("exp_1")).reshape(1).astype(jnp.int32)
    w_down0 = w_down[0].reshape(2, -1, dim)

    tokens_wide = wide(tokens)
    normed = rms_scale(tokens_wide, moe_gain).astype(jnp.bfloat16)
    lane = lax.broadcasted_iota(jnp.int32, (rows, LANES), 1)
    numer = jnp.where(expert_ids[:, :1] == lane, gate_nums[:, :1], 0) + jnp.where(
        expert_ids[:, 1:] == lane, gate_nums[:, 1:], 0
    )
    packed = jnp.concatenate([normed, numer.astype(jnp.bfloat16)], axis=1)

    column = jnp.concatenate([packed, swap(packed, "exp_0")], 0)
    w_gu = w_gate_up[0].transpose(1, 2, 0).reshape(4, -1, dim)
    w_qkv2 = w_qkv.transpose(1, 2, 0).reshape(-1, dim)

    def experts(planes):
        other = swap(jnp.concatenate(planes, 0) if len(planes) > 1 else planes[0], "exp_1")
        mine, theirs = expert_call(planes, other, w_gu, w_down0, me)
        chip = added(mine, swap(theirs, "exp_1"))
        cut = rows * len(planes)
        across = swap(chip[cut:], "exp_0")
        return [
            (chip[i * rows : (i + 1) * rows], across[i * rows : (i + 1) * rows])
            for i in range(len(planes))
        ]

    up1, down1 = shift(column, 1), shift(column, -1)
    (up1, down1), (w_gu, w_qkv2) = tied((up1, down1), (w_gu, w_qkv2))
    up2, down2 = shift(up1, 1), shift(down1, -1)
    own_terms, b1, a1 = experts([column, up1, down1])
    up3, down3 = shift(up2, 1), shift(down2, -1)
    b2, a2 = experts([up2, down2])
    far_up, far_down = shift(up3[:rows], 1), shift(down3[rows:], -1)
    b3, a3 = experts([up3, down3])
    (far_terms,) = experts([jnp.concatenate([far_up, far_down], 0)])
    above = jnp.concatenate([added(*t) for t in (far_terms, a3, a2, a1)], 0)
    blank = jnp.zeros((rows, dim), jnp.bfloat16)
    below = jnp.concatenate([blank, *(added(*t) for t in (b3, b2, b1))], 0)
    from_below, from_above = ring_scatter(above, below, rows)
    moe_total = wide(own_terms[0]) + wide(own_terms[1]) + wide(from_below) + wide(from_above)
    mixed = (tokens_wide + moe_total).astype(jnp.bfloat16)

    mixed_wide = wide(mixed)
    attn_in = rms_scale(mixed_wide, attn_gain).astype(jnp.bfloat16)
    head = q_gain.shape[0]
    heads = w_qkv.shape[2] // head

    def project(parts):
        q, kv = project_call(parts, w_qkv2, q_gain, k_gain, heads)
        beside = swap(kv, "exp_0")
        return q, jnp.concatenate([kv, beside], 0)

    half = rows // 2
    up1, down1 = shift(attn_in, 1), shift(attn_in, -1)
    up2, down2 = shift(up1, 1), shift(down1, -1)
    up3, down3 = shift(up2, 1), shift(down2, -1)
    q_a, kv_a = project([attn_in, up1, down1, up2, down2])
    far = (shift(up3[:half], 1), shift(down3[half:], -1))
    kv_a = lax.all_gather(kv_a, "exp_1", axis=0, tiled=True)
    far, kv_a = tied(far, kv_a)
    q_b, kv_b = project([up3, down3, jnp.concatenate(far, 0)])
    kvs = [kv_a, kv_b, swap(kv_b, "exp_1")]
    piece = attend_call([q_a, q_b], kvs, w_out, heads, rows)
    from_below, from_above = ring_scatter(
        jnp.concatenate([piece[7], *piece[6:1:-2]], 0),
        jnp.concatenate([blank, *piece[5:0:-2]], 0),
        rows,
    )
    attended = (
        mixed_wide + (wide(piece[0]) + wide(from_below) + wide(from_above))
    ).astype(jnp.bfloat16)
    return (mixed, attended)


def solution(mesh):
    torus = Mesh(
        mesh.devices.reshape(mesh.shape["set"], 2, 2, mesh.shape["seq"]),
        ("set", "exp_0", "exp_1", "seq"),
    )
    in_specs = (
        P(SET_EXP_SEQ, None),
        P(SET_EXP_SEQ, None),
        P(SET_EXP_SEQ, None),
        P(),
        P(EXP, None, None, "seq"),
        P(EXP, "seq", None),
        P(),
        P(None, None, "seq"),
        P(),
        P(),
        P("seq", None),
    )
    out_specs = (P(SET_EXP_SEQ, None), P(SET_EXP_SEQ, None))

    return jax.shard_map(shards, mesh=torus, in_specs=in_specs, out_specs=out_specs, check_vma=False)
```

```python
import math

import jax
import jax.numpy as jnp
from jax import lax
from jax.experimental import pallas as pl
from jax.experimental.pallas import tpu as pltpu
from jax.sharding import Mesh
from jax.sharding import PartitionSpec as P


LANES = 128
EXP = ("exp_0", "exp_1")
SET_EXP_SEQ = ("set", "exp_0", "exp_1", "seq")


def swap(value, axis):
    return lax.ppermute(value, axis, [(0, 1), (1, 0)])


def shift(value, step):
    n = lax.axis_size("seq")
    return lax.ppermute(value, "seq", [(i, (i + step) % n) for i in range(n)])


def wide(value):
    return value.astype(jnp.float32)


def added(*values):
    total = wide(values[0])
    for v in values[1:]:
        total = total + wide(v)
    return total.astype(jnp.bfloat16)


def tied(first, second):
    return lax.optimization_barrier((first, second))


def rms_scale(values, gain):
    return values * lax.rsqrt(jnp.mean(values * values, axis=-1, keepdims=True) + 1e-06) * gain


def ring_scatter(above, below, rows):
    blank = jnp.zeros((rows, above.shape[1]), jnp.bfloat16)

    def step(i, carry):
        up, down = carry
        at_up = lax.dynamic_slice_in_dim(above, i * rows, rows)
        at_down = lax.dynamic_slice_in_dim(below, i * rows, rows)
        return shift(added(at_up, up), 1), shift(added(at_down, down), -1)

    return lax.fori_loop(0, above.shape[0] // rows, step, (blank, blank))


ANY = pl.BlockSpec(memory_space=pl.ANY)
FAR = pl.BlockSpec(memory_space=pltpu.HBM)


TRANS = (((1,), (1,)), ((), ()))


def expert_call(mine, other, w_gate_up, w_down, me):
    n = len(mine)
    plane = mine[0].shape[0]
    half = plane // 2
    _, fb, dim = w_gate_up.shape
    ff = 2 * fb
    cols = mine[0].shape[1]
    m1 = n * plane
    m = 2 * m1
    kc = 512
    nk = dim // kc

    def kernel(me_ref, *refs):
        xs, (ox, wgu, wd, out_mine, out_other) = refs[:n], refs[n : n + 5]
        x_s, wgu_s, wd_s, acc, h_s, sh_s, sx, sg, sd = refs[n + 5 :]

        def w_copy(k):
            return pltpu.make_async_copy(wgu.at[k], wgu_s.at[k], sg.at[k])

        copies = []
        for i in range(n):
            for b in range(2):
                src = pl.ds(b * half, half)
                dst = (b * n + i) * half
                copies.append(
                    pltpu.make_async_copy(
                        xs[i].at[src], x_s.at[pl.ds(dst, half)], sx.at[0, 2 * i + b]
                    )
                )
                src = pl.ds(i * plane + b * half, half)
                copies.append(
                    pltpu.make_async_copy(
                        ox.at[src], x_s.at[pl.ds(m1 + dst, half)], sx.at[1, 2 * i + b]
                    )
                )
        d_copy = pltpu.make_async_copy(wd, wd_s, sd)
        for c in copies:
            c.start()
        for k in range(4):
            w_copy(k).start()
        d_copy.start()
        for c in copies:
            c.wait()
        nums = x_s[:, dim:].astype(jnp.float32)
        here = lax.broadcasted_iota(jnp.int32, nums.shape, 1) == me_ref[0]
        share = jnp.sum(jnp.where(here, nums, 0.0), axis=1, keepdims=True) / jnp.sum(
            nums, axis=1, keepdims=True
        )
        sh_s[...] = jnp.broadcast_to(share, sh_s.shape)

        def step(k, carry):
            w_copy(k).wait()
            acc[k] = lax.dot_general(
                x_s[:, :dim], wgu_s[k], TRANS, preferred_element_type=jnp.float32
            )
            return carry

        lax.fori_loop(0, 4, step, 0)
        for b in range(2):
            gate = acc[b]
            h_s[b] = (gate / (1.0 + jnp.exp(-gate)) * acc[2 + b]).astype(jnp.bfloat16)
        d_copy.wait()

        def down(k, carry):
            at = pl.ds(pl.multiple_of(k * kc, kc), kc)
            y = jnp.dot(h_s[0], wd_s[0, :, at], preferred_element_type=jnp.float32) + jnp.dot(
                h_s[1], wd_s[1, :, at], preferred_element_type=jnp.float32
            )
            y = (y * sh_s[:, :1]).astype(jnp.bfloat16)
            out_mine[:, at] = y[:m1]
            out_other[:, at] = y[m1:]
            return carry

        lax.fori_loop(0, nk, down, 0)

    return pl.pallas_call(
        kernel,
        out_shape=[jax.ShapeDtypeStruct((m1, dim), jnp.bfloat16)] * 2,
        in_specs=[pl.BlockSpec(memory_space=pltpu.SMEM)] + [ANY] * (n + 1) + [FAR, FAR],
        out_specs=[pl.BlockSpec(memory_space=pltpu.VMEM)] * 2,
        scratch_shapes=[
            pltpu.VMEM((m, cols), jnp.bfloat16),
            pltpu.VMEM((4, fb, dim), jnp.bfloat16),
            pltpu.VMEM((2, fb, dim), jnp.bfloat16),
            pltpu.VMEM((4, m, fb), jnp.float32),
            pltpu.VMEM((2, m, fb), jnp.bfloat16),
            pltpu.VMEM((m, LANES), jnp.float32),
            pltpu.SemaphoreType.DMA((2, 2 * n)),
            pltpu.SemaphoreType.DMA((4,)),
            pltpu.SemaphoreType.DMA,
        ],
        compiler_params=pltpu.CompilerParams(vmem_limit_bytes=50 * 2**20),
        cost_estimate=pl.CostEstimate(
            flops=6 * m * dim * ff, bytes_accessed=6 * dim * ff + 4 * m * dim, transcendentals=m * ff
        ),
        name="expert",
    )(me, *mine, other, w_gate_up, w_down)


def project_call(parts, w, q_gain, k_gain, heads):
    n = len(parts)
    sizes = [p.shape[0] for p in parts]
    m = sum(sizes)
    _, dim, width = w.shape
    cols = 3 * width
    head = width // heads
    kc = 512
    nk = dim // kc

    def kernel(*refs):
        xs, (w_ref, qg, kg, q_out, kv_out, x_s, w_s, acc, sx, sw) = refs[:n], refs[n:]

        def x_copy(i):
            return pltpu.make_async_copy(
                xs[i], x_s.at[pl.ds(sum(sizes[:i]), sizes[i])], sx.at[i]
            )

        def w_copy(k):
            at = pl.ds(pl.multiple_of(k * kc, kc), kc)
            return pltpu.make_async_copy(w_ref.at[:, at], w_s.at[:, at], sw.at[k])

        for i in range(n):
            x_copy(i).start()
        for k in range(nk):
            w_copy(k).start()
        acc[...] = jnp.zeros_like(acc)
        for i in range(n):
            x_copy(i).wait()

        def step(k, carry):
            at = pl.ds(pl.multiple_of(k * kc, kc), kc)
            w_copy(k).wait()
            x = x_s[:, at]
            for g in range(3):
                acc[:, g * width : (g + 1) * width] += jnp.dot(
                    x, w_s[g, at, :], preferred_element_type=jnp.float32
                )
            return carry

        lax.fori_loop(0, nk, step, 0)
        for i in range(heads):
            at = slice(i * head, (i + 1) * head)
            q_out[:, at] = rms_scale(acc[:, at], qg[...]).astype(jnp.bfloat16)
            at_k = slice(width + i * head, width + (i + 1) * head)
            kv_out[:, at] = rms_scale(acc[:, at_k], kg[...]).astype(jnp.bfloat16)
        kv_out[:, width:] = acc[:, 2 * width :].astype(jnp.bfloat16)

    vmem = pl.BlockSpec(memory_space=pltpu.VMEM)
    return pl.pallas_call(
        kernel,
        out_shape=[
            jax.ShapeDtypeStruct((m, width), jnp.bfloat16),
            jax.ShapeDtypeStruct((m, 2 * width), jnp.bfloat16),
        ],
        in_specs=[ANY] * n + [FAR, vmem, vmem],
        out_specs=[vmem, vmem],
        scratch_shapes=[
            pltpu.VMEM((m, dim), jnp.bfloat16),
            pltpu.VMEM((3, dim, width), jnp.bfloat16),
            pltpu.VMEM((m, cols), jnp.float32),
            pltpu.SemaphoreType.DMA((n,)),
            pltpu.SemaphoreType.DMA((nk,)),
        ],
        compiler_params=pltpu.CompilerParams(vmem_limit_bytes=58 * 2**20),
        cost_estimate=pl.CostEstimate(
            flops=2 * m * dim * cols, bytes_accessed=2 * dim * cols + 2 * m * dim, transcendentals=0
        ),
        name="project",
    )(*parts, w, q_gain.reshape(1, -1), k_gain.reshape(1, -1))


def attend_call(queries, kvs, w_out, heads, rows):
    nq, nv = len(queries), len(kvs)
    m = sum(q.shape[0] for q in queries)
    t = sum(k.shape[0] for k in kvs)
    width = queries[0].shape[1]
    head = width // heads
    dim = w_out.shape[1]
    planes = m // rows
    scale_factor = 1.0 / math.sqrt(head)

    def kernel(*refs):
        qs, ks, w_ref = refs[:nq], refs[nq : nq + nv], refs[nq + nv]
        outs = refs[nq + nv + 1 : nq + nv + 1 + planes]
        q_s, kv_s, w_s, o_s, sq, sk, sw = refs[nq + nv + 1 + planes :]
        copies = []
        at = 0
        for i, k in enumerate(ks):
            copies.append(pltpu.make_async_copy(k, kv_s.at[pl.ds(at, k.shape[0])], sk.at[i]))
            at += k.shape[0]
        at = 0
        for i, q in enumerate(qs):
            copies.append(pltpu.make_async_copy(q, q_s.at[pl.ds(at, q.shape[0])], sq.at[i]))
            at += q.shape[0]
        w_copy = pltpu.make_async_copy(w_ref, w_s, sw)
        for c in copies:
            c.start()
        w_copy.start()
        for c in copies:
            c.wait()
        block = 128

        def rows_step(b, carry):
            r = pl.ds(pl.multiple_of(b * block, block), block)
            for i in range(heads):
                at = slice(i * head, (i + 1) * head)
                scores = (
                    lax.dot_general(
                        q_s[r, at], kv_s[:, at], TRANS, preferred_element_type=jnp.float32
                    )
                    * scale_factor
                )
                probs = jnp.exp(scores)
                denom = jnp.sum(probs, axis=1, keepdims=True)
                num = jnp.dot(
                    probs.astype(jnp.bfloat16),
                    kv_s[:, width + i * head : width + (i + 1) * head],
                    preferred_element_type=jnp.float32,
                )
                o_s[r, at] = (num / denom).astype(jnp.bfloat16)
            return carry

        lax.fori_loop(0, m // block, rows_step, 0)
        w_copy.wait()
        kc = 512

        def out_step(k, carry):
            cols = pl.ds(pl.multiple_of(k * kc, kc), kc)
            y = jnp.dot(o_s[...], w_s[:, cols], preferred_element_type=jnp.float32)
            y = y.astype(jnp.bfloat16)
            for i in range(planes):
                outs[i][:, cols] = y[i * rows : (i + 1) * rows]
            return carry

        lax.fori_loop(0, dim // kc, out_step, 0)

    return pl.pallas_call(
        kernel,
        out_shape=[jax.ShapeDtypeStruct((rows, dim), jnp.bfloat16)] * planes,
        in_specs=[ANY] * (nq + nv) + [FAR],
        out_specs=[pl.BlockSpec(memory_space=pltpu.VMEM)] * planes,
        scratch_shapes=[
            pltpu.VMEM((m, width), jnp.bfloat16),
            pltpu.VMEM((t, 2 * width), jnp.bfloat16),
            pltpu.VMEM(w_out.shape, jnp.bfloat16),
            pltpu.VMEM((m, width), jnp.bfloat16),
            pltpu.SemaphoreType.DMA((nq,)),
            pltpu.SemaphoreType.DMA((nv,)),
            pltpu.SemaphoreType.DMA,
        ],
        compiler_params=pltpu.CompilerParams(vmem_limit_bytes=32 * 2**20),
        cost_estimate=pl.CostEstimate(
            flops=4 * m * t * width + 2 * m * width * dim,
            bytes_accessed=2 * (t * 2 * width + width * dim + m * dim),
            transcendentals=m * t * heads,
        ),
        name="attend",
    )(*queries, *kvs, w_out)


def shards(
    tokens,
    expert_ids,
    gate_nums,
    moe_gain,
    w_gate_up,
    w_down,
    attn_gain,
    w_qkv,
    q_gain,
    k_gain,
    w_out,
):
    rows, dim = tokens.shape
    me = (lax.axis_index("exp_0") * 2 + lax.axis_index("exp_1")).reshape(1).astype(jnp.int32)
    w_down0 = w_down[0].reshape(2, -1, dim)

    tokens_wide = wide(tokens)
    normed = rms_scale(tokens_wide, moe_gain).astype(jnp.bfloat16)
    lane = lax.broadcasted_iota(jnp.int32, (rows, LANES), 1)
    numer = jnp.where(expert_ids[:, :1] == lane, gate_nums[:, :1], 0) + jnp.where(
        expert_ids[:, 1:] == lane, gate_nums[:, 1:], 0
    )
    packed = jnp.concatenate([normed, numer.astype(jnp.bfloat16)], axis=1)

    w_gu = w_gate_up[0].transpose(1, 2, 0).reshape(4, -1, dim)
    w_qkv3 = w_qkv.transpose(1, 0, 2)
    beside = swap(packed, "exp_0")
    up_a, down_a = shift(packed, 1), shift(packed, -1)
    up_b, down_b = shift(beside, 1), shift(beside, -1)
    column = jnp.concatenate([packed, beside], 0)
    up1, down1 = jnp.concatenate([up_a, up_b], 0), jnp.concatenate([down_a, down_b], 0)

    def experts(planes):
        other = swap(jnp.concatenate(planes, 0) if len(planes) > 1 else planes[0], "exp_1")
        mine, theirs = expert_call(planes, other, w_gu, w_down0, me)
        got = swap(theirs, "exp_1")
        cut = rows * len(planes)
        across = swap(added(mine[cut:], got[cut:]), "exp_0")
        return [
            tuple(t[i * rows : (i + 1) * rows] for t in (mine, got, across))
            for i in range(len(planes))
        ]

    up2, down2 = shift(up1, 1), shift(down1, -1)
    own_terms, b1, a1 = experts([column, up1, down1])
    up3, down3 = shift(up2, 1), shift(down2, -1)
    b2, a2 = experts([up2, down2])
    far_up, far_down = shift(up3[:rows], 1), shift(down3[rows:], -1)
    b3, a3 = experts([up3, down3])
    (far_terms,) = experts([jnp.concatenate([far_up, far_down], 0)])
    above = jnp.concatenate([added(*t) for t in (far_terms, a3, a2, a1)], 0)
    blank = jnp.zeros((rows, dim), jnp.bfloat16)
    below = jnp.concatenate([blank, *(added(*t) for t in (b3, b2, b1))], 0)
    from_below, from_above = ring_scatter(above, below, rows)
    moe_total = sum(wide(t) for t in (*own_terms, from_below, from_above))
    mixed = (tokens_wide + moe_total).astype(jnp.bfloat16)

    mixed_wide = wide(mixed)
    attn_in = rms_scale(mixed_wide, attn_gain).astype(jnp.bfloat16)
    head = q_gain.shape[0]
    heads = w_qkv.shape[2] // head

    def project(parts):
        q, kv = project_call(parts, w_qkv3, q_gain, k_gain, heads)
        beside = swap(kv, "exp_0")
        return q, jnp.concatenate([kv, beside], 0)

    half = rows // 2
    up1, down1 = shift(attn_in, 1), shift(attn_in, -1)
    up2, down2 = shift(up1, 1), shift(down1, -1)
    up3, down3 = shift(up2, 1), shift(down2, -1)
    q_a, kv_a = project([attn_in, up1, down1, up2, down2])
    far = (shift(up3[:half], 1), shift(down3[half:], -1))
    kv_a = lax.all_gather(kv_a, "exp_1", axis=0, tiled=True)
    far, kv_a = tied(far, kv_a)
    q_b, kv_b = project([up3, down3, jnp.concatenate(far, 0)])
    kvs = [kv_a, kv_b, swap(kv_b, "exp_1")]
    piece = attend_call([q_a, q_b], kvs, w_out, heads, rows)
    from_below, from_above = ring_scatter(
        jnp.concatenate([piece[7], *piece[6:1:-2]], 0),
        jnp.concatenate([blank, *piece[5:0:-2]], 0),
        rows,
    )
    attended = (
        mixed_wide + (wide(piece[0]) + wide(from_below) + wide(from_above))
    ).astype(jnp.bfloat16)
    return (mixed, attended)


def solution(mesh):
    torus = Mesh(
        mesh.devices.reshape(mesh.shape["set"], 2, 2, mesh.shape["seq"]),
        ("set", "exp_0", "exp_1", "seq"),
    )
    in_specs = (
        P(SET_EXP_SEQ, None),
        P(SET_EXP_SEQ, None),
        P(SET_EXP_SEQ, None),
        P(),
        P(EXP, None, None, "seq"),
        P(EXP, "seq", None),
        P(),
        P(None, None, "seq"),
        P(),
        P(),
        P("seq", None),
    )
    out_specs = (P(SET_EXP_SEQ, None), P(SET_EXP_SEQ, None))

    return jax.shard_map(shards, mesh=torus, in_specs=in_specs, out_specs=out_specs, check_vma=False)
```

```python
import math

import jax
import jax.numpy as jnp
from jax import lax
from jax.experimental import pallas as pl
from jax.experimental.pallas import tpu as pltpu
from jax.sharding import Mesh
from jax.sharding import PartitionSpec as P


LANES = 128
EXP = ("exp_0", "exp_1")
SET_EXP_SEQ = ("set", "exp_0", "exp_1", "seq")


def swap(value, axis):
    return lax.ppermute(value, axis, [(0, 1), (1, 0)])


def shift(value, step):
    n = lax.axis_size("seq")
    return lax.ppermute(value, "seq", [(i, (i + step) % n) for i in range(n)])


def wide(value):
    return value.astype(jnp.float32)


def added(*values):
    total = wide(values[0])
    for v in values[1:]:
        total = total + wide(v)
    return total.astype(jnp.bfloat16)


def tied(first, second):
    return lax.optimization_barrier((first, second))


def rms_scale(values, gain):
    return values * lax.rsqrt(jnp.mean(values * values, axis=-1, keepdims=True) + 1e-06) * gain


def ring_scatter(above, below, rows):
    blank = jnp.zeros((rows, above.shape[1]), jnp.bfloat16)

    def step(i, carry):
        up, down = carry
        at_up = lax.dynamic_slice_in_dim(above, i * rows, rows)
        at_down = lax.dynamic_slice_in_dim(below, i * rows, rows)
        return shift(added(at_up, up), 1), shift(added(at_down, down), -1)

    return lax.fori_loop(0, above.shape[0] // rows, step, (blank, blank))


ANY = pl.BlockSpec(memory_space=pl.ANY)
FAR = pl.BlockSpec(memory_space=pltpu.HBM)


TRANS = (((1,), (1,)), ((), ()))


def expert_call(mine, other, w_gate_up, w_down, me):
    n = len(mine)
    plane = mine[0].shape[0]
    half = plane // 2
    _, fb, dim = w_gate_up.shape
    ff = 2 * fb
    cols = mine[0].shape[1]
    m1 = n * plane
    m = 2 * m1
    kc = 512
    nk = dim // kc

    def kernel(me_ref, *refs):
        xs, (ox, wgu, wd, out_mine, out_other) = refs[:n], refs[n : n + 5]
        x_s, wgu_s, wd_s, acc, h_s, sh_s, sx, sg, sd = refs[n + 5 :]

        def w_copy(k):
            return pltpu.make_async_copy(wgu.at[k], wgu_s.at[k], sg.at[k])

        copies = []
        for i in range(n):
            for b in range(2):
                src = pl.ds(b * half, half)
                dst = (b * n + i) * half
                copies.append(
                    pltpu.make_async_copy(
                        xs[i].at[src], x_s.at[pl.ds(dst, half)], sx.at[0, 2 * i + b]
                    )
                )
                src = pl.ds(i * plane + b * half, half)
                copies.append(
                    pltpu.make_async_copy(
                        ox.at[src], x_s.at[pl.ds(m1 + dst, half)], sx.at[1, 2 * i + b]
                    )
                )
        d_copy = pltpu.make_async_copy(wd, wd_s, sd)
        for c in copies:
            c.start()
        for k in range(4):
            w_copy(k).start()
        d_copy.start()
        for c in copies:
            c.wait()
        nums = x_s[:, dim:].astype(jnp.float32)
        here = lax.broadcasted_iota(jnp.int32, nums.shape, 1) == me_ref[0]
        share = jnp.sum(jnp.where(here, nums, 0.0), axis=1, keepdims=True) / jnp.sum(
            nums, axis=1, keepdims=True
        )
        sh_s[...] = jnp.broadcast_to(share, sh_s.shape)

        def step(k, carry):
            w_copy(k).wait()
            acc[k] = lax.dot_general(
                x_s[:, :dim], wgu_s[k], TRANS, preferred_element_type=jnp.float32
            )
            return carry

        lax.fori_loop(0, 4, step, 0)
        for b in range(2):
            gate = acc[b]
            h_s[b] = (gate / (1.0 + jnp.exp(-gate)) * acc[2 + b]).astype(jnp.bfloat16)
        d_copy.wait()

        def down(k, carry):
            at = pl.ds(pl.multiple_of(k * kc, kc), kc)
            y = jnp.dot(h_s[0], wd_s[0, :, at], preferred_element_type=jnp.float32) + jnp.dot(
                h_s[1], wd_s[1, :, at], preferred_element_type=jnp.float32
            )
            y = (y * sh_s[:, :1]).astype(jnp.bfloat16)
            out_mine[:, at] = y[:m1]
            out_other[:, at] = y[m1:]
            return carry

        lax.fori_loop(0, nk, down, 0)

    return pl.pallas_call(
        kernel,
        out_shape=[jax.ShapeDtypeStruct((m1, dim), jnp.bfloat16)] * 2,
        in_specs=[pl.BlockSpec(memory_space=pltpu.SMEM)] + [ANY] * (n + 1) + [FAR, FAR],
        out_specs=[pl.BlockSpec(memory_space=pltpu.VMEM)] * 2,
        scratch_shapes=[
            pltpu.VMEM((m, cols), jnp.bfloat16),
            pltpu.VMEM((4, fb, dim), jnp.bfloat16),
            pltpu.VMEM((2, fb, dim), jnp.bfloat16),
            pltpu.VMEM((4, m, fb), jnp.float32),
            pltpu.VMEM((2, m, fb), jnp.bfloat16),
            pltpu.VMEM((m, LANES), jnp.float32),
            pltpu.SemaphoreType.DMA((2, 2 * n)),
            pltpu.SemaphoreType.DMA((4,)),
            pltpu.SemaphoreType.DMA,
        ],
        compiler_params=pltpu.CompilerParams(vmem_limit_bytes=50 * 2**20),
        cost_estimate=pl.CostEstimate(
            flops=6 * m * dim * ff, bytes_accessed=6 * dim * ff + 4 * m * dim, transcendentals=m * ff
        ),
        name="expert",
    )(me, *mine, other, w_gate_up, w_down)


def project_call(parts, w, q_gain, k_gain, heads):
    n = len(parts)
    sizes = [p.shape[0] for p in parts]
    m = sum(sizes)
    _, dim, width = w.shape
    cols = 3 * width
    head = width // heads
    kc = 512
    nk = dim // kc

    def kernel(*refs):
        xs, (w_ref, qg, kg, q_out, kv_out, x_s, w_s, acc, sx, sw) = refs[:n], refs[n:]

        def x_copy(i):
            return pltpu.make_async_copy(
                xs[i], x_s.at[pl.ds(sum(sizes[:i]), sizes[i])], sx.at[i]
            )

        def w_copy(k):
            at = pl.ds(pl.multiple_of(k * kc, kc), kc)
            return pltpu.make_async_copy(w_ref.at[:, at], w_s.at[:, at], sw.at[k])

        for i in range(n):
            x_copy(i).start()
        for k in range(nk):
            w_copy(k).start()
        acc[...] = jnp.zeros_like(acc)
        for i in range(n):
            x_copy(i).wait()

        def step(k, carry):
            at = pl.ds(pl.multiple_of(k * kc, kc), kc)
            w_copy(k).wait()
            x = x_s[:, at]
            for g in range(3):
                acc[:, g * width : (g + 1) * width] += jnp.dot(
                    x, w_s[g, at, :], preferred_element_type=jnp.float32
                )
            return carry

        lax.fori_loop(0, nk, step, 0)
        for i in range(heads):
            at = slice(i * head, (i + 1) * head)
            q_out[:, at] = rms_scale(acc[:, at], qg[...]).astype(jnp.bfloat16)
            at_k = slice(width + i * head, width + (i + 1) * head)
            kv_out[:, at] = rms_scale(acc[:, at_k], kg[...]).astype(jnp.bfloat16)
        kv_out[:, width:] = acc[:, 2 * width :].astype(jnp.bfloat16)

    vmem = pl.BlockSpec(memory_space=pltpu.VMEM)
    return pl.pallas_call(
        kernel,
        out_shape=[
            jax.ShapeDtypeStruct((m, width), jnp.bfloat16),
            jax.ShapeDtypeStruct((m, 2 * width), jnp.bfloat16),
        ],
        in_specs=[ANY] * n + [FAR, vmem, vmem],
        out_specs=[vmem, vmem],
        scratch_shapes=[
            pltpu.VMEM((m, dim), jnp.bfloat16),
            pltpu.VMEM((3, dim, width), jnp.bfloat16),
            pltpu.VMEM((m, cols), jnp.float32),
            pltpu.SemaphoreType.DMA((n,)),
            pltpu.SemaphoreType.DMA((nk,)),
        ],
        compiler_params=pltpu.CompilerParams(vmem_limit_bytes=16 * 2**20),
        cost_estimate=pl.CostEstimate(
            flops=2 * m * dim * cols, bytes_accessed=2 * dim * cols + 2 * m * dim, transcendentals=0
        ),
        name="project",
    )(*parts, w, q_gain.reshape(1, -1), k_gain.reshape(1, -1))


def attend_call(queries, kvs, w_out, heads, rows):
    nq, nv = len(queries), len(kvs)
    m = sum(q.shape[0] for q in queries)
    t = sum(k.shape[0] for k in kvs)
    width = queries[0].shape[1]
    head = width // heads
    dim = w_out.shape[1]
    planes = m // rows
    scale_factor = 1.0 / math.sqrt(head)

    def kernel(*refs):
        qs, ks, w_ref = refs[:nq], refs[nq : nq + nv], refs[nq + nv]
        outs = refs[nq + nv + 1 : nq + nv + 1 + planes]
        q_s, kv_s, w_s, o_s, sq, sk, sw = refs[nq + nv + 1 + planes :]
        copies = []
        at = 0
        for i, k in enumerate(ks):
            copies.append(pltpu.make_async_copy(k, kv_s.at[pl.ds(at, k.shape[0])], sk.at[i]))
            at += k.shape[0]
        at = 0
        for i, q in enumerate(qs):
            copies.append(pltpu.make_async_copy(q, q_s.at[pl.ds(at, q.shape[0])], sq.at[i]))
            at += q.shape[0]
        w_copy = pltpu.make_async_copy(w_ref, w_s, sw)
        for c in copies:
            c.start()
        w_copy.start()
        for c in copies:
            c.wait()
        block = 128

        def rows_step(b, carry):
            r = pl.ds(pl.multiple_of(b * block, block), block)
            for i in range(heads):
                at = slice(i * head, (i + 1) * head)
                scores = (
                    lax.dot_general(
                        q_s[r, at], kv_s[:, at], TRANS, preferred_element_type=jnp.float32
                    )
                    * scale_factor
                )
                probs = jnp.exp(scores)
                denom = jnp.sum(probs, axis=1, keepdims=True)
                num = jnp.dot(
                    probs.astype(jnp.bfloat16),
                    kv_s[:, width + i * head : width + (i + 1) * head],
                    preferred_element_type=jnp.float32,
                )
                o_s[r, at] = (num / denom).astype(jnp.bfloat16)
            return carry

        lax.fori_loop(0, m // block, rows_step, 0)
        w_copy.wait()
        kc = 512

        def out_step(k, carry):
            cols = pl.ds(pl.multiple_of(k * kc, kc), kc)
            y = jnp.dot(o_s[...], w_s[:, cols], preferred_element_type=jnp.float32)
            y = y.astype(jnp.bfloat16)
            for i in range(planes):
                outs[i][:, cols] = y[i * rows : (i + 1) * rows]
            return carry

        lax.fori_loop(0, dim // kc, out_step, 0)

    return pl.pallas_call(
        kernel,
        out_shape=[jax.ShapeDtypeStruct((rows, dim), jnp.bfloat16)] * planes,
        in_specs=[ANY] * (nq + nv) + [FAR],
        out_specs=[pl.BlockSpec(memory_space=pltpu.VMEM)] * planes,
        scratch_shapes=[
            pltpu.VMEM((m, width), jnp.bfloat16),
            pltpu.VMEM((t, 2 * width), jnp.bfloat16),
            pltpu.VMEM(w_out.shape, jnp.bfloat16),
            pltpu.VMEM((m, width), jnp.bfloat16),
            pltpu.SemaphoreType.DMA((nq,)),
            pltpu.SemaphoreType.DMA((nv,)),
            pltpu.SemaphoreType.DMA,
        ],
        compiler_params=pltpu.CompilerParams(vmem_limit_bytes=32 * 2**20),
        cost_estimate=pl.CostEstimate(
            flops=4 * m * t * width + 2 * m * width * dim,
            bytes_accessed=2 * (t * 2 * width + width * dim + m * dim),
            transcendentals=m * t * heads,
        ),
        name="attend",
    )(*queries, *kvs, w_out)


def shards(
    tokens,
    expert_ids,
    gate_nums,
    moe_gain,
    w_gate_up,
    w_down,
    attn_gain,
    w_qkv,
    q_gain,
    k_gain,
    w_out,
):
    rows, dim = tokens.shape
    me = (lax.axis_index("exp_0") * 2 + lax.axis_index("exp_1")).reshape(1).astype(jnp.int32)
    w_down0 = w_down[0].reshape(2, -1, dim)

    tokens_wide = wide(tokens)
    normed = rms_scale(tokens_wide, moe_gain).astype(jnp.bfloat16)
    lane = lax.broadcasted_iota(jnp.int32, (rows, LANES), 1)
    numer = jnp.where(expert_ids[:, :1] == lane, gate_nums[:, :1], 0) + jnp.where(
        expert_ids[:, 1:] == lane, gate_nums[:, 1:], 0
    )
    packed = jnp.concatenate([normed, numer.astype(jnp.bfloat16)], axis=1)

    w_gu = w_gate_up[0].transpose(1, 2, 0).reshape(4, -1, dim)
    w_qkv3 = w_qkv.transpose(1, 0, 2)
    beside = swap(packed, "exp_0")
    up_a, down_a = shift(packed, 1), shift(packed, -1)
    up_b, down_b = shift(beside, 1), shift(beside, -1)
    column = jnp.concatenate([packed, beside], 0)
    up1, down1 = jnp.concatenate([up_a, up_b], 0), jnp.concatenate([down_a, down_b], 0)

    def experts(planes):
        other = swap(jnp.concatenate(planes, 0) if len(planes) > 1 else planes[0], "exp_1")
        mine, theirs = expert_call(planes, other, w_gu, w_down0, me)
        got = swap(theirs, "exp_1")
        cut = rows * len(planes)
        across = swap(added(mine[cut:], got[cut:]), "exp_0")
        return [
            tuple(t[i * rows : (i + 1) * rows] for t in (mine, got, across))
            for i in range(len(planes))
        ]

    up2, down2 = shift(up1, 1), shift(down1, -1)
    (own_terms,) = experts([column])
    b1, a1 = experts([up1, down1])
    up3, down3 = shift(up2, 1), shift(down2, -1)
    b2, a2 = experts([up2, down2])
    far_up, far_down = shift(up3[:rows], 1), shift(down3[rows:], -1)
    b3, a3 = experts([up3, down3])
    (far_terms,) = experts([jnp.concatenate([far_up, far_down], 0)])
    above = jnp.concatenate([added(*t) for t in (far_terms, a3, a2, a1)], 0)
    blank = jnp.zeros((rows, dim), jnp.bfloat16)
    below = jnp.concatenate([blank, *(added(*t) for t in (b3, b2, b1))], 0)
    from_below, from_above = ring_scatter(above, below, rows)
    moe_total = sum(wide(t) for t in (*own_terms, from_below, from_above))
    mixed = (tokens_wide + moe_total).astype(jnp.bfloat16)

    mixed_wide = wide(mixed)
    attn_in = rms_scale(mixed_wide, attn_gain).astype(jnp.bfloat16)
    head = q_gain.shape[0]
    heads = w_qkv.shape[2] // head

    def project(parts):
        q, kv = project_call(parts, w_qkv3, q_gain, k_gain, heads)
        beside = swap(kv, "exp_0")
        return q, jnp.concatenate([kv, beside], 0)

    up1, down1 = shift(attn_in, 1), shift(attn_in, -1)
    up2, down2 = shift(up1, 1), shift(down1, -1)
    up3, down3 = shift(up2, 1), shift(down2, -1)
    q_a, kv_a = project([attn_in, up1, down1, up2, down2])
    far = shift(up3, 1)
    kv_a = lax.all_gather(kv_a, "exp_1", axis=0, tiled=True)
    far, kv_a = tied(far, kv_a)
    q_b, kv_b = project([up3, down3, far])
    kvs = [kv_a, kv_b, swap(kv_b, "exp_1")]
    piece = attend_call([q_a, q_b], kvs, w_out, heads, rows)
    from_below, from_above = ring_scatter(
        jnp.concatenate([piece[7], *piece[6:1:-2]], 0),
        jnp.concatenate([blank, *piece[5:0:-2]], 0),
        rows,
    )
    attended = (
        mixed_wide + (wide(piece[0]) + wide(from_below) + wide(from_above))
    ).astype(jnp.bfloat16)
    return (mixed, attended)


def solution(mesh):
    torus = Mesh(
        mesh.devices.reshape(mesh.shape["set"], 2, 2, mesh.shape["seq"]),
        ("set", "exp_0", "exp_1", "seq"),
    )
    in_specs = (
        P(SET_EXP_SEQ, None),
        P(SET_EXP_SEQ, None),
        P(SET_EXP_SEQ, None),
        P(),
        P(EXP, None, None, "seq"),
        P(EXP, "seq", None),
        P(),
        P(None, None, "seq"),
        P(),
        P(),
        P("seq", None),
    )
    out_specs = (P(SET_EXP_SEQ, None), P(SET_EXP_SEQ, None))

    return jax.shard_map(shards, mesh=torus, in_specs=in_specs, out_specs=out_specs, check_vma=False)
```

```python
import math

import jax
import jax.numpy as jnp
from jax import lax
from jax.experimental import pallas as pl
from jax.experimental.pallas import tpu as pltpu
from jax.sharding import Mesh
from jax.sharding import PartitionSpec as P


LANES = 128
EXP = ("exp_0", "exp_1")
SET_EXP_SEQ = ("set", "exp_0", "exp_1", "seq")


def swap(value, axis):
    return lax.ppermute(value, axis, [(0, 1), (1, 0)])


def shift(value, step):
    n = lax.axis_size("seq")
    return lax.ppermute(value, "seq", [(i, (i + step) % n) for i in range(n)])


def wide(value):
    return value.astype(jnp.float32)


def added(*values):
    total = wide(values[0])
    for v in values[1:]:
        total = total + wide(v)
    return total.astype(jnp.bfloat16)


def tied(first, second):
    return lax.optimization_barrier((first, second))


def rms_scale(values, gain):
    return values * lax.rsqrt(jnp.mean(values * values, axis=-1, keepdims=True) + 1e-06) * gain


def ring_scatter(above, below, rows):
    blank = jnp.zeros((rows, above.shape[1]), jnp.bfloat16)

    def step(i, carry):
        up, down = carry
        at_up = lax.dynamic_slice_in_dim(above, i * rows, rows)
        at_down = lax.dynamic_slice_in_dim(below, i * rows, rows)
        return shift(added(at_up, up), 1), shift(added(at_down, down), -1)

    return lax.fori_loop(0, above.shape[0] // rows, step, (blank, blank))


ANY = pl.BlockSpec(memory_space=pl.ANY)
FAR = pl.BlockSpec(memory_space=pltpu.HBM)


TRANS = (((1,), (1,)), ((), ()))


def expert_call(mine, other, w_gate_up, w_down, me):
    n = len(mine)
    plane = mine[0].shape[0]
    half = plane // 2
    _, fb, dim = w_gate_up.shape
    ff = 2 * fb
    cols = mine[0].shape[1]
    m1 = n * plane
    m = 2 * m1
    kc = 512
    nk = dim // kc

    def kernel(me_ref, *refs):
        xs, (ox, wgu, wd, out_mine, out_other) = refs[:n], refs[n : n + 5]
        x_s, wgu_s, wd_s, acc, h_s, sh_s, sx, sg, sd = refs[n + 5 :]

        def w_copy(k):
            return pltpu.make_async_copy(wgu.at[k], wgu_s.at[k], sg.at[k])

        copies = []
        for i in range(n):
            for b in range(2):
                src = pl.ds(b * half, half)
                dst = (b * n + i) * half
                copies.append(
                    pltpu.make_async_copy(
                        xs[i].at[src], x_s.at[pl.ds(dst, half)], sx.at[0, 2 * i + b]
                    )
                )
                src = pl.ds(i * plane + b * half, half)
                copies.append(
                    pltpu.make_async_copy(
                        ox.at[src], x_s.at[pl.ds(m1 + dst, half)], sx.at[1, 2 * i + b]
                    )
                )
        d_copy = pltpu.make_async_copy(wd, wd_s, sd)
        for c in copies:
            c.start()
        for k in range(4):
            w_copy(k).start()
        d_copy.start()
        for c in copies:
            c.wait()
        nums = x_s[:, dim:].astype(jnp.float32)
        here = lax.broadcasted_iota(jnp.int32, nums.shape, 1) == me_ref[0]
        share = jnp.sum(jnp.where(here, nums, 0.0), axis=1, keepdims=True) / jnp.sum(
            nums, axis=1, keepdims=True
        )
        sh_s[...] = jnp.broadcast_to(share, sh_s.shape)

        def step(k, carry):
            w_copy(k).wait()
            acc[k] = lax.dot_general(
                x_s[:, :dim], wgu_s[k], TRANS, preferred_element_type=jnp.float32
            )
            return carry

        lax.fori_loop(0, 4, step, 0)
        for b in range(2):
            gate = acc[b]
            h_s[b] = (gate / (1.0 + jnp.exp(-gate)) * acc[2 + b]).astype(jnp.bfloat16)
        d_copy.wait()

        def down(k, carry):
            at = pl.ds(pl.multiple_of(k * kc, kc), kc)
            y = jnp.dot(h_s[0], wd_s[0, :, at], preferred_element_type=jnp.float32) + jnp.dot(
                h_s[1], wd_s[1, :, at], preferred_element_type=jnp.float32
            )
            y = (y * sh_s[:, :1]).astype(jnp.bfloat16)
            out_mine[:, at] = y[:m1]
            out_other[:, at] = y[m1:]
            return carry

        lax.fori_loop(0, nk, down, 0)

    return pl.pallas_call(
        kernel,
        out_shape=[jax.ShapeDtypeStruct((m1, dim), jnp.bfloat16)] * 2,
        in_specs=[pl.BlockSpec(memory_space=pltpu.SMEM)] + [ANY] * (n + 1) + [FAR, FAR],
        out_specs=[pl.BlockSpec(memory_space=pltpu.VMEM)] * 2,
        scratch_shapes=[
            pltpu.VMEM((m, cols), jnp.bfloat16),
            pltpu.VMEM((4, fb, dim), jnp.bfloat16),
            pltpu.VMEM((2, fb, dim), jnp.bfloat16),
            pltpu.VMEM((4, m, fb), jnp.float32),
            pltpu.VMEM((2, m, fb), jnp.bfloat16),
            pltpu.VMEM((m, LANES), jnp.float32),
            pltpu.SemaphoreType.DMA((2, 2 * n)),
            pltpu.SemaphoreType.DMA((4,)),
            pltpu.SemaphoreType.DMA,
        ],
        compiler_params=pltpu.CompilerParams(vmem_limit_bytes=50 * 2**20),
        cost_estimate=pl.CostEstimate(
            flops=6 * m * dim * ff, bytes_accessed=6 * dim * ff + 4 * m * dim, transcendentals=m * ff
        ),
        name="expert",
    )(me, *mine, other, w_gate_up, w_down)


def project_call(parts, w, q_gain, k_gain, heads):
    n = len(parts)
    sizes = [p.shape[0] for p in parts]
    m = sum(sizes)
    _, dim, width = w.shape
    cols = 3 * width
    head = width // heads
    kc = 512
    nk = dim // kc

    def kernel(*refs):
        xs, (w_ref, qg, kg, q_out, kv_out, x_s, w_s, acc, sx, sw) = refs[:n], refs[n:]

        def x_copy(i):
            return pltpu.make_async_copy(
                xs[i], x_s.at[pl.ds(sum(sizes[:i]), sizes[i])], sx.at[i]
            )

        def w_copy(k):
            at = pl.ds(pl.multiple_of(k * kc, kc), kc)
            return pltpu.make_async_copy(w_ref.at[:, at], w_s.at[:, at], sw.at[k])

        for i in range(n):
            x_copy(i).start()
        for k in range(nk):
            w_copy(k).start()
        acc[...] = jnp.zeros_like(acc)
        for i in range(n):
            x_copy(i).wait()

        def step(k, carry):
            at = pl.ds(pl.multiple_of(k * kc, kc), kc)
            w_copy(k).wait()
            x = x_s[:, at]
            for g in range(3):
                acc[:, g * width : (g + 1) * width] += jnp.dot(
                    x, w_s[g, at, :], preferred_element_type=jnp.float32
                )
            return carry

        lax.fori_loop(0, nk, step, 0)
        for i in range(heads):
            at = slice(i * head, (i + 1) * head)
            q_out[:, at] = rms_scale(acc[:, at], qg[...]).astype(jnp.bfloat16)
            at_k = slice(width + i * head, width + (i + 1) * head)
            kv_out[:, at] = rms_scale(acc[:, at_k], kg[...]).astype(jnp.bfloat16)
        kv_out[:, width:] = acc[:, 2 * width :].astype(jnp.bfloat16)

    vmem = pl.BlockSpec(memory_space=pltpu.VMEM)
    return pl.pallas_call(
        kernel,
        out_shape=[
            jax.ShapeDtypeStruct((m, width), jnp.bfloat16),
            jax.ShapeDtypeStruct((m, 2 * width), jnp.bfloat16),
        ],
        in_specs=[ANY] * n + [FAR, vmem, vmem],
        out_specs=[vmem, vmem],
        scratch_shapes=[
            pltpu.VMEM((m, dim), jnp.bfloat16),
            pltpu.VMEM((3, dim, width), jnp.bfloat16),
            pltpu.VMEM((m, cols), jnp.float32),
            pltpu.SemaphoreType.DMA((n,)),
            pltpu.SemaphoreType.DMA((nk,)),
        ],
        compiler_params=pltpu.CompilerParams(vmem_limit_bytes=16 * 2**20),
        cost_estimate=pl.CostEstimate(
            flops=2 * m * dim * cols, bytes_accessed=2 * dim * cols + 2 * m * dim, transcendentals=0
        ),
        name="project",
    )(*parts, w, q_gain.reshape(1, -1), k_gain.reshape(1, -1))


def attend_call(queries, kvs, w_out, heads, rows):
    nq, nv = len(queries), len(kvs)
    m = sum(q.shape[0] for q in queries)
    t = sum(k.shape[0] for k in kvs)
    width = queries[0].shape[1]
    head = width // heads
    dim = w_out.shape[1]
    planes = m // rows
    scale_factor = 1.0 / math.sqrt(head)

    def kernel(*refs):
        qs, ks, w_ref = refs[:nq], refs[nq : nq + nv], refs[nq + nv]
        outs = refs[nq + nv + 1 : nq + nv + 1 + planes]
        q_s, kv_s, w_s, o_s, sq, sk, sw = refs[nq + nv + 1 + planes :]
        copies = []
        at = 0
        for i, k in enumerate(ks):
            copies.append(pltpu.make_async_copy(k, kv_s.at[pl.ds(at, k.shape[0])], sk.at[i]))
            at += k.shape[0]
        at = 0
        for i, q in enumerate(qs):
            copies.append(pltpu.make_async_copy(q, q_s.at[pl.ds(at, q.shape[0])], sq.at[i]))
            at += q.shape[0]
        w_copy = pltpu.make_async_copy(w_ref, w_s, sw)
        for c in copies:
            c.start()
        w_copy.start()
        for c in copies:
            c.wait()
        block = 128

        def rows_step(b, carry):
            r = pl.ds(pl.multiple_of(b * block, block), block)
            for i in range(heads):
                at = slice(i * head, (i + 1) * head)
                scores = (
                    lax.dot_general(
                        q_s[r, at], kv_s[:, at], TRANS, preferred_element_type=jnp.float32
                    )
                    * scale_factor
                )
                probs = jnp.exp(scores)
                denom = jnp.sum(probs, axis=1, keepdims=True)
                num = jnp.dot(
                    probs.astype(jnp.bfloat16),
                    kv_s[:, width + i * head : width + (i + 1) * head],
                    preferred_element_type=jnp.float32,
                )
                o_s[r, at] = (num / denom).astype(jnp.bfloat16)
            return carry

        lax.fori_loop(0, m // block, rows_step, 0)
        w_copy.wait()
        kc = 512

        def out_step(k, carry):
            cols = pl.ds(pl.multiple_of(k * kc, kc), kc)
            y = jnp.dot(o_s[...], w_s[:, cols], preferred_element_type=jnp.float32)
            y = y.astype(jnp.bfloat16)
            for i in range(planes):
                outs[i][:, cols] = y[i * rows : (i + 1) * rows]
            return carry

        lax.fori_loop(0, dim // kc, out_step, 0)

    return pl.pallas_call(
        kernel,
        out_shape=[jax.ShapeDtypeStruct((rows, dim), jnp.bfloat16)] * planes,
        in_specs=[ANY] * (nq + nv) + [FAR],
        out_specs=[pl.BlockSpec(memory_space=pltpu.VMEM)] * planes,
        scratch_shapes=[
            pltpu.VMEM((m, width), jnp.bfloat16),
            pltpu.VMEM((t, 2 * width), jnp.bfloat16),
            pltpu.VMEM(w_out.shape, jnp.bfloat16),
            pltpu.VMEM((m, width), jnp.bfloat16),
            pltpu.SemaphoreType.DMA((nq,)),
            pltpu.SemaphoreType.DMA((nv,)),
            pltpu.SemaphoreType.DMA,
        ],
        compiler_params=pltpu.CompilerParams(vmem_limit_bytes=32 * 2**20),
        cost_estimate=pl.CostEstimate(
            flops=4 * m * t * width + 2 * m * width * dim,
            bytes_accessed=2 * (t * 2 * width + width * dim + m * dim),
            transcendentals=m * t * heads,
        ),
        name="attend",
    )(*queries, *kvs, w_out)


def shards(
    tokens,
    expert_ids,
    gate_nums,
    moe_gain,
    w_gate_up,
    w_down,
    attn_gain,
    w_qkv,
    q_gain,
    k_gain,
    w_out,
):
    rows, dim = tokens.shape
    me = (lax.axis_index("exp_0") * 2 + lax.axis_index("exp_1")).reshape(1).astype(jnp.int32)
    w_down0 = w_down[0].reshape(2, -1, dim)

    tokens_wide = wide(tokens)
    normed = rms_scale(tokens_wide, moe_gain).astype(jnp.bfloat16)
    lane = lax.broadcasted_iota(jnp.int32, (rows, LANES), 1)
    numer = jnp.where(expert_ids[:, :1] == lane, gate_nums[:, :1], 0) + jnp.where(
        expert_ids[:, 1:] == lane, gate_nums[:, 1:], 0
    )
    packed = jnp.concatenate([normed, numer.astype(jnp.bfloat16)], axis=1)

    w_gu = w_gate_up[0].transpose(1, 2, 0).reshape(4, -1, dim)
    w_qkv3 = w_qkv.transpose(1, 0, 2)
    beside = swap(packed, "exp_0")
    up_a, down_a = shift(packed, 1), shift(packed, -1)
    up_b, down_b = shift(beside, 1), shift(beside, -1)
    column = jnp.concatenate([packed, beside], 0)
    up1, down1 = jnp.concatenate([up_a, up_b], 0), jnp.concatenate([down_a, down_b], 0)

    def experts(planes):
        other = swap(jnp.concatenate(planes, 0) if len(planes) > 1 else planes[0], "exp_1")
        mine, theirs = expert_call(planes, other, w_gu, w_down0, me)
        got = swap(theirs, "exp_1")
        cut = rows * len(planes)
        across = swap(added(mine[cut:], got[cut:]), "exp_0")
        return [
            tuple(t[i * rows : (i + 1) * rows] for t in (mine, got, across))
            for i in range(len(planes))
        ]

    up2, down2 = shift(up1, 1), shift(down1, -1)
    (own_terms,) = experts([column])
    b1, a1 = experts([up1, down1])
    up3, down3 = shift(up2, 1), shift(down2, -1)
    b2, a2 = experts([up2, down2])
    far_up, far_down = shift(up3[:rows], 1), shift(down3[rows:], -1)
    b3, a3 = experts([up3, down3])
    (far_terms,) = experts([jnp.concatenate([far_up, far_down], 0)])
    above = jnp.concatenate([added(*t) for t in (far_terms, a3, a2, a1)], 0)
    blank = jnp.zeros((rows, dim), jnp.bfloat16)
    below = jnp.concatenate([blank, *(added(*t) for t in (b3, b2, b1))], 0)
    from_below, from_above = ring_scatter(above, below, rows)
    moe_total = sum(wide(t) for t in (*own_terms, from_below, from_above))
    mixed = (tokens_wide + moe_total).astype(jnp.bfloat16)

    mixed_wide = wide(mixed)
    attn_in = rms_scale(mixed_wide, attn_gain).astype(jnp.bfloat16)
    head = q_gain.shape[0]
    heads = w_qkv.shape[2] // head

    def project(parts):
        q, kv = project_call(parts, w_qkv3, q_gain, k_gain, heads)
        beside = swap(kv, "exp_0")
        return q, jnp.concatenate([kv, beside], 0)

    up1, down1 = shift(attn_in, 1), shift(attn_in, -1)
    up2, down2 = shift(up1, 1), shift(down1, -1)
    up3, down3 = shift(up2, 1), shift(down2, -1)
    q_a, kv_a = project([attn_in, up1, down1])
    kv_a = lax.all_gather(kv_a, "exp_1", axis=0, tiled=True)
    (up3, down3), kv_a = tied((up3, down3), kv_a)
    far = shift(up3, 1)
    q_b, kv_b = project([up2, down2, up3, down3, far])
    kvs = [kv_a, kv_b, swap(kv_b, "exp_1")]
    piece = attend_call([q_a, q_b], kvs, w_out, heads, rows)
    from_below, from_above = ring_scatter(
        jnp.concatenate([piece[7], *piece[6:1:-2]], 0),
        jnp.concatenate([blank, *piece[5:0:-2]], 0),
        rows,
    )
    attended = (
        mixed_wide + (wide(piece[0]) + wide(from_below) + wide(from_above))
    ).astype(jnp.bfloat16)
    return (mixed, attended)


def solution(mesh):
    torus = Mesh(
        mesh.devices.reshape(mesh.shape["set"], 2, 2, mesh.shape["seq"]),
        ("set", "exp_0", "exp_1", "seq"),
    )
    in_specs = (
        P(SET_EXP_SEQ, None),
        P(SET_EXP_SEQ, None),
        P(SET_EXP_SEQ, None),
        P(),
        P(EXP, None, None, "seq"),
        P(EXP, "seq", None),
        P(),
        P(None, None, "seq"),
        P(),
        P(),
        P("seq", None),
    )
    out_specs = (P(SET_EXP_SEQ, None), P(SET_EXP_SEQ, None))

    return jax.shard_map(shards, mesh=torus, in_specs=in_specs, out_specs=out_specs, check_vma=False)
```
